128 devices in a mesh: dom: 16 (over z, y), sub: 4 (over x), rep: 2 (over core).
Axes of the slice: x: 4, y: 4, z: 4, core: 2. Of those that a mesh axis runs over, the one named last changes fastest.
Arguments:
- queries: bfloat16 [8192, 768], P(('dom', 'sub', 'rep')), may hold values from -5 to 5
- codebook: bfloat16 [192, 16, 4], replicated, may hold values from -1 to 1
- probes: int32 [8192, 8], P(('dom', 'sub', 'rep')), may hold values from 0 to 255, all different within a row; in each aligned block of 64 rows (0 to 63, 64 to 127, ...) at most 4 rows name the same one
- codes: int32 [256, 192, 2048], P(('dom', 'sub'), None, 'rep'), may hold values from 0 to 15
- part_sizes: int32 [256], P(('dom', 'sub')), may hold values from 1536 to 2048
Outputs:
- best_scores: float32 [8192, 100], P(('dom', 'sub', 'rep'))
The draws below stay inside these ranges and needn't reach their ends.
Inputs may be any that keep to these rules, and one draw needn't show every extreme that they name: `probes`: each row names 8 different partitions. Among the rows of one device no partition is named more than 4 times, and in every draw some partition is named exactly 4 times by one device's rows.
All inputs are finite; a program needn't handle non-finite values.
Results may differ from the reference program's by a relative error of at most 0.00066.
Values may be sent and summed in bfloat16 or wider, within the bound.
A program may use at most 256 MiB of HBM per device.

```python
import math
import jax
import jax.numpy as jnp
import numpy as np
from jax import lax

D = 768
SUBS = 192
CENT = 16
SUBDIM = 4
QDEV = 64
SLOTS = 2048
NPROBE = 8
TOPK = 100
NQ = 8192
PARTS_SIZE = 256
CAP = 4
N_DOM = 16
N_SUB = 4
N_REP = 2


def common_parts(key):
    centre_key = jax.random.fold_in(key, 11)
    favour_key = jax.random.fold_in(key, 12)
    centre = jnp.clip(jax.random.normal(centre_key, (D,), jnp.float32), -3.0, 3.0)
    favoured = jax.random.randint(favour_key, (SUBS,), 0, CENT).astype(jnp.int32)
    return (centre, favoured)


def draw_codebook(key, part):
    centre, favoured = common_parts(key)
    jitter_key = jax.random.fold_in(key, 13)
    jitter = jnp.clip(jax.random.normal(jitter_key, (SUBS, CENT, SUBDIM), jnp.float32), -4.0, 4.0) * D ** (-0.5)
    raised = (jnp.arange(CENT, dtype=jnp.int32)[None, :] == favoured[:, None]).astype(jnp.float32)
    shaped = centre.reshape(SUBS, SUBDIM)
    centroids = jitter + 0.55 * D ** (-0.5) * raised[:, :, None] * shaped[:, None, :]
    return centroids.astype(jnp.bfloat16)


def draw_queries(key, part):
    centre, favoured = common_parts(key)
    spread_key = jax.random.fold_in(key, 14)
    spread = jnp.clip(jax.random.normal(spread_key, (NQ, D), jnp.float32), -4.0, 4.0)
    vectors = 0.5 * centre[None, :] + 0.85 * spread
    return vectors.astype(jnp.bfloat16)


def draw_codes(key, part):
    centre, favoured = common_parts(key)
    uniform_codes = jax.random.randint(jax.random.fold_in(key, 16), (PARTS_SIZE, SUBS, SLOTS), 0, CENT).astype(jnp.int32)
    altered = jax.random.randint(jax.random.fold_in(key, 17), (PARTS_SIZE, SUBS, SLOTS), 0, 8).astype(jnp.int32)
    planted_count = max(1, PARTS_SIZE // 32)
    ranking = jax.random.permutation(jax.random.fold_in(key, 18), PARTS_SIZE).astype(jnp.int32)
    planted = ranking < planted_count
    span_length = min(SLOTS // 4, 2 * TOPK)
    which_half = jax.random.randint(jax.random.fold_in(key, 19), (PARTS_SIZE,), 0, 2).astype(jnp.int32)
    offsets = jax.random.randint(jax.random.fold_in(key, 20), (PARTS_SIZE,), 0, SLOTS // 4 - span_length + 1).astype(jnp.int32)
    cluster_start = which_half * (SLOTS // 2) + offsets
    slot_ids = jnp.arange(SLOTS, dtype=jnp.int32)
    inside = (slot_ids[None, :] >= cluster_start[:, None]) & (slot_ids[None, :] < cluster_start[:, None] + span_length) & planted[:, None]
    use_favoured = inside[:, None, :] & (altered != 0)
    return jnp.where(use_favoured, favoured[None, :, None], uniform_codes).astype(jnp.int32)


def with_ends(array, own_key, least, top_value):
    extent = array.shape
    spot = [jax.random.randint(jax.random.fold_in(own_key, axis), (), 0, extent[axis]) for axis in range(len(extent))]
    array = array.at[tuple(spot)].set(least)
    longest = extent.index(max(extent))
    spot[longest] = (spot[longest] + 1) % extent[longest]
    return array.at[tuple(spot)].set(top_value)


def routed_block(key, own, number, rows, count, top, bound, slope):
    sequence = jax.random.permutation(key, count)
    crowded, usual = load_shares(count, rows * top, bound, slope, True), load_shares(count, rows * top, bound, slope, False)
    places = jnp.arange(count)

    def named(lengths, rotation):
        used = int((lengths > 0).sum())
        fixed = max(1, used // 4)
        shifted = fixed + (places - fixed + rotation * (used - fixed)) % max(1, count - fixed)
        return jnp.zeros((count,), jnp.int32).at[sequence[jnp.where(places < fixed, places, shifted)]].set(jnp.asarray(lengths, jnp.int32))

    lengths = jnp.where(number % 4 == 0, named(crowded, number // 4), named(usual, number - number // 4 - 1))
    mixed = jax.random.permutation(jax.random.fold_in(own, 3), count)
    source_of, sink = mixed[0:count // 2 * 2:2], mixed[1:count // 2 * 2:2]
    slack = jnp.minimum(lengths[source_of] - 1, bound - lengths[sink]) // 2
    slack = jnp.where((source_of == sequence[0]) | (sink == sequence[0]) | (lengths[sink] == 0), 0, jnp.maximum(slack, 0))
    shifted = jax.random.randint(jax.random.fold_in(own, 4), (count // 2,), 0, 1 << 20) % (slack + 1)
    lengths = lengths.at[source_of].add(-shifted).at[sink].add(shifted)
    members = jnp.searchsorted(jnp.cumsum(lengths), jnp.arange(rows * top), side="right").astype(jnp.int32)
    table = members.reshape(top, rows).T
    table = table[jax.random.permutation(jax.random.fold_in(own, 1), rows)]
    rotation = jax.random.randint(jax.random.fold_in(own, 2), (rows, 1), 0, top)
    return jnp.take_along_axis(table, (jnp.arange(top)[None, :] + rotation) % top, axis=1)


def load_shares(count, total, limit, skew, full):
    loads = [(1 << 20) // math.isqrt(grade ** skew) + 1 for grade in range(1, count + 1)]
    largest = limit if full else min(limit, max(-(-total // count), total * loads[0] // sum(loads)))
    least = 1 if total - largest >= count - 1 else 0
    given, spare = [largest] + [least] * (count - 1), total - largest - least * (count - 1)
    while spare > 0:
        free = [i for i in range(1, count) if given[i] < largest] or [i for i in range(1, count) if given[i] < limit]
        mass, remaining = sum([loads[i] for i in free]), spare
        for i in free:
            extra = min(limit - given[i], max(1, remaining * loads[i] // mass), spare)
            given[i] = given[i] + extra
            spare = spare - extra
    return np.array(given)


def setup_inputs(seed: int = 0) -> dict:
    key_of = jax.random.split(jax.random.key(seed), 6)
    queries = draw_queries(jax.random.fold_in(key_of[5], 71), 0)
    codebook = draw_codebook(jax.random.fold_in(key_of[5], 71), 0)
    probes_keys = jax.random.split(jax.random.fold_in(key_of[2], 1), NQ // QDEV)
    probes_turns = jax.random.permutation(jax.random.fold_in(key_of[2], 3), NQ // QDEV)
    probes = jax.vmap(lambda own, number: routed_block(jax.random.fold_in(key_of[2], 2), own, number, QDEV, PARTS_SIZE, NPROBE, CAP, 2))(probes_keys, probes_turns).reshape((NQ, NPROBE))
    codes = draw_codes(jax.random.fold_in(key_of[5], 71), 0)
    part_sizes = with_ends(jax.random.randint(key_of[4], (PARTS_SIZE,), SLOTS * 3 // 4, SLOTS + 1), jax.random.fold_in(key_of[4], 1), SLOTS * 3 // 4, SLOTS).astype(jnp.int32)
    return dict(queries=queries, codebook=codebook, probes=probes, codes=codes, part_sizes=part_sizes)


MASKED = -1.0e30


def build_tables(queries, codebook):
    n_rows = queries.shape[0]
    pieces = queries.astype(jnp.float32).reshape(n_rows, SUBS, SUBDIM)
    tables = jnp.einsum('rsj,scj->rsc', pieces, codebook.astype(jnp.float32))
    return tables.reshape(n_rows, SUBS * CENT).astype(jnp.bfloat16)


def reference(queries, codebook, probes, codes, part_sizes):
    tables = build_tables(queries, codebook)
    row_limit = N_DOM * N_SUB * N_REP * CAP
    slot_ids = jnp.arange(SLOTS, dtype=jnp.int32)
    centroid_ids = jnp.arange(CENT, dtype=jnp.int32)
    probe_ids = jnp.arange(NPROBE, dtype=jnp.int32)

    def one_part(candidates, part_id):
        probed = jnp.any(probes == part_id, axis=1)
        (row_index,) = jnp.nonzero(probed, size=row_limit, fill_value=NQ)
        row_index = row_index.astype(jnp.int32)
        safe_rows = jnp.minimum(row_index, NQ - 1)
        probe_slot = jnp.sum(jnp.where(probes[safe_rows] == part_id, probe_ids[None, :], 0), axis=1).astype(jnp.int32)
        chosen = tables[safe_rows].astype(jnp.float32)
        onehot = (codes[part_id][:, None, :] == centroid_ids[None, :, None]).astype(jnp.float32).reshape(SUBS * CENT, SLOTS)
        scores = jnp.dot(chosen, onehot, preferred_element_type=jnp.float32)
        scores = jnp.where(slot_ids[None, :] < part_sizes[part_id], scores, MASKED)
        best_vals = lax.top_k(scores, TOPK)[0]
        candidates = candidates.at[row_index, probe_slot].set(best_vals, mode='drop')
        return candidates, None

    candidates = jnp.full((NQ, NPROBE, TOPK), MASKED, dtype=jnp.float32)
    candidates, _ = lax.scan(one_part, candidates, jnp.arange(PARTS_SIZE, dtype=jnp.int32))
    return lax.top_k(candidates.reshape(NQ, NPROBE * TOPK), TOPK)[0]
```

```python
import functools

import jax
import jax.numpy as jnp
from jax import lax
from jax.experimental import pallas as pl
from jax.experimental.pallas import tpu as pltpu
from jax.sharding import PartitionSpec as P

TOPK = 100
MASKED = -1e30
RANKS = 128
LANES = 128
SUBL = 8


def batcher(n):
    pairs = []

    def merge(lo, cnt, r):
        step = r * 2
        if step < cnt:
            merge(lo, cnt, step)
            merge(lo + r, cnt, step)
            for i in range(lo + r, lo + cnt - r, step):
                pairs.append((i, i + r))
        else:
            pairs.append((lo, lo + r))

    def sort(lo, cnt):
        if cnt > 1:
            m = cnt // 2
            sort(lo, m)
            sort(lo + m, m)
            merge(lo, cnt, 1)

    sort(0, n)
    return pairs


SORT32 = batcher(32)


def exchange(x, pairs):
    for i, j in pairs:
        a, b = x[i], x[j]
        x[i] = jnp.maximum(a, b)
        x[j] = jnp.minimum(a, b)
    return x


def clean(x):
    d = len(x) // 2
    while d:
        exchange(x, [(i, i + d) for i in range(len(x)) if not i & d])
        d //= 2
    return x


def prep_kernel(n_cap, q_ref, probes_ref, send_ref, idx_ref):
    rows, width = q_ref.shape
    slots = send_ref.shape[0]
    n = lax.broadcasted_iota(jnp.int32, (rows, slots), 1)
    part = n // n_cap
    rank_of = (n % n_cap).astype(jnp.float32)
    probes = probes_ref[...]
    named = part == probes[:, 0:1]
    for k in range(1, probes.shape[1]):
        named = named | (part == probes[:, k : k + 1])
    before = (
        lax.broadcasted_iota(jnp.int32, (rows, rows), 0) > lax.broadcasted_iota(jnp.int32, (rows, rows), 1)
    ).astype(jnp.float32).astype(jnp.bfloat16)
    rank = jnp.dot(before, named.astype(jnp.float32).astype(jnp.bfloat16), preferred_element_type=jnp.float32)
    chosen = jnp.where(named & (rank == rank_of), 1.0, 0.0)
    nf = n.astype(jnp.float32)
    for k in range(probes.shape[1]):
        hit = jnp.where(part == probes[:, k : k + 1], chosen, 0.0)
        idx_ref[:, k : k + 1] = jnp.sum(hit * nf, axis=1, keepdims=True).astype(jnp.int32)
    a = lax.broadcasted_iota(jnp.int32, (width, width), 0)
    b = lax.broadcasted_iota(jnp.int32, (width, width), 1)
    groups = width // 4
    j = (b >= groups).astype(jnp.int32) + (b >= 2 * groups).astype(jnp.int32) + (b >= 3 * groups).astype(jnp.int32)
    perm = jnp.where(a == (b - groups * j) * 4 + j, 1.0, 0.0).astype(jnp.bfloat16)
    moved = jnp.dot(q_ref[...], perm, preferred_element_type=jnp.float32).astype(jnp.bfloat16)
    picked = lax.dot_general(
        chosen.astype(jnp.bfloat16), moved, (((0,), (0,)), ((), ())), preferred_element_type=jnp.float32
    )
    send_ref[...] = picked.astype(jnp.bfloat16)


def prep(queries, probes, n_slots, n_cap):
    return pl.pallas_call(
        functools.partial(prep_kernel, n_cap),
        out_shape=(
            jax.ShapeDtypeStruct((n_slots, queries.shape[1]), jnp.bfloat16),
            jax.ShapeDtypeStruct(probes.shape, jnp.int32),
        ),
        in_specs=[pl.BlockSpec(memory_space=pltpu.VMEM)] * 2,
        out_specs=[pl.BlockSpec(memory_space=pltpu.VMEM)] * 2,
        compiler_params=pltpu.CompilerParams(vmem_limit_bytes=40 << 20),
        name="prep",
    )(queries, probes)


def sort_block(s_ref, x_ref, b, h):
    groups = s_ref.shape[1] // 32

    @pl.loop(0, groups)
    def _(g):
        x = exchange([s_ref[b, g * 32 + i] for i in range(32)], SORT32)
        for i in range(32):
            s_ref[b, g * 32 + i] = x[i]

    @pl.loop(0, groups // 2)
    def _(g):
        base = g * 64
        low = []
        high = []
        for i in range(32):
            u, v = s_ref[b, base + i], s_ref[b, base + 63 - i]
            high.append(jnp.maximum(u, v))
            low.append(jnp.minimum(u, v))
        clean(high)
        clean(low)
        for i in range(32):
            s_ref[b, base + i] = high[i]
            s_ref[b, base + 32 + i] = low[i]

    @pl.loop(0, groups // 4)
    def _(g):
        base = g * 128

        @pl.loop(0, 32, unroll=8)
        def _(i):
            u0, u1 = s_ref[b, base + i], s_ref[b, base + 32 + i]
            v0, v1 = s_ref[b, base + 127 - i], s_ref[b, base + 95 - i]
            h0, h1 = jnp.maximum(u0, v0), jnp.maximum(u1, v1)
            l0, l1 = jnp.minimum(u0, v0), jnp.minimum(u1, v1)
            x_ref[h, i] = jnp.maximum(h0, h1)
            x_ref[h, 32 + i] = jnp.minimum(h0, h1)
            x_ref[h, 64 + i] = jnp.maximum(l0, l1)
            x_ref[h, 96 + i] = jnp.minimum(l0, l1)

        @pl.loop(0, 4)
        def _(k):
            x = clean([x_ref[h, k * 32 + i] for i in range(32)])
            for i in range(32):
                s_ref[b, base + k * 32 + i] = x[i]

    @pl.loop(0, 32, unroll=8)
    def _(i):
        t = [jnp.maximum(s_ref[b, i + 32 * k], s_ref[b, 255 - i - 32 * k]) for k in range(4)]
        clean(t)
        for k in range(4):
            x_ref[h, i + 32 * k] = t[k]

    @pl.loop(0, 4)
    def _(k):
        x = clean([x_ref[h, k * 32 + i] for i in range(32)])
        for i in range(32):
            x_ref[h, k * 32 + i] = x[i]


def merge_pair(x_ref, b0, b1, level):
    bit = 1 << level
    lower = (lax.broadcasted_iota(jnp.int32, (SUBL, LANES), 0) & bit) == 0

    def joined(i, m):
        first = jnp.where(lower, x_ref[b0, i], x_ref[b1, i])
        second = jnp.where(lower, pltpu.roll(x_ref[b0, m], SUBL - bit, 0), pltpu.roll(x_ref[b1, m], bit, 0))
        return jnp.maximum(first, second)

    @pl.loop(0, 64, unroll=4)
    def _(i):
        m = 127 - i
        s, t = joined(i, m), joined(m, i)
        x_ref[b0, i] = s
        x_ref[b0, m] = t

    @pl.loop(0, 32, unroll=8)
    def _(i):
        t = clean([x_ref[b0, i + 32 * k] for k in range(4)])
        for k in range(4):
            x_ref[b0, i + 32 * k] = t[k]

    @pl.loop(0, 4)
    def _(k):
        x = clean([x_ref[b0, k * 32 + i] for i in range(32)])
        for i in range(32):
            x_ref[b0, k * 32 + i] = x[i]


def score_kernel(n_cap, sizes_ref, table_ref, q_ref, own_ref, peer_ref, out_ref, d_ref, s_ref, x_ref, z_ref):
    p = pl.program_id(0)
    groups, half = own_ref.shape[1:]
    part_dev = pl.num_programs(0)
    tiles = half // LANES

    @pl.loop(0, groups // 16)
    def _(g):
        rows = pl.ds(pl.multiple_of(g * 16, 16), 16)
        tab = [table_ref[j, rows, :] for j in range(4)]
        for t in range(2 * tiles):
            ref = own_ref if t < tiles else peer_ref
            c = ref[0, rows, (t % tiles) * LANES : (t % tiles + 1) * LANES]
            for j in range(4):
                val = jnp.take_along_axis(tab[j], c, axis=1)
                d_ref[pl.ds(pl.multiple_of(j * groups + g * 16, 16), 16), t * LANES : (t + 1) * LANES] = val.astype(
                    jnp.bfloat16
                )

    all_rows = q_ref.shape[0]
    m = lax.broadcasted_iota(jnp.int32, (256, all_rows), 0)
    src = (m // 128) * 32 + m % 32
    want = src * (part_dev * n_cap) + p * n_cap + (m % 128) // 32
    pick = jnp.where(lax.broadcasted_iota(jnp.int32, (256, all_rows), 1) == want, 1.0, 0.0).astype(jnp.bfloat16)
    mine = jnp.dot(pick, q_ref[...], preferred_element_type=jnp.float32).astype(jnp.bfloat16)

    @pl.loop(0, 2 * half // 256)
    def _(t):
        cols = pl.ds(pl.multiple_of(t * 256, 256), 256)
        sc = jnp.dot(mine, d_ref[:, cols], preferred_element_type=jnp.float32)
        sc = sc.T
        per_half = half // 256
        which = t // per_half
        slot = lax.broadcasted_iota(jnp.int32, (256, LANES), 0) + (t - which * per_half) * 256
        ok = slot < sizes_ref[which, p]
        for h in range(2):
            blk = jnp.where(ok, sc[:, h * LANES : (h + 1) * LANES], MASKED)
            s_ref[h, pl.ds(t * 32, 32)] = blk.reshape(32, SUBL, LANES)

    for h in range(2):
        sort_block(s_ref, x_ref, h, p * 2 + h)

    @pl.when(p == part_dev - 1)
    def _():
        for b in range(0, 8, 2):
            merge_pair(x_ref, b, b + 1, 2)
        for b in range(0, 8, 4):
            merge_pair(x_ref, b, b + 2, 1)
        merge_pair(x_ref, 0, 4, 0)
        z_ref[...] = x_ref[0].reshape(RANKS * SUBL, LANES)
        for blk in range(8):
            u = 4 * (blk & 1) + (blk & 2) + (blk >> 2)
            got = z_ref[pl.ds(u, RANKS, stride=SUBL), :].T
            for r in range(n_cap):
                base = (blk & 1) * 32 * 16 + (blk >> 1) * n_cap + r
                out_ref[pl.ds(base, 32, stride=16), :] = got[r * 32 : (r + 1) * 32, :]


def score(sizes, table, rows, own, peer, n_cap):
    part_dev, groups, half = own.shape
    n_rows, width = rows.shape
    blk = pl.BlockSpec((1, groups, half), lambda p: (p, 0, 0))
    return pl.pallas_call(
        functools.partial(score_kernel, n_cap),
        grid=(part_dev,),
        out_shape=jax.ShapeDtypeStruct((n_rows, RANKS), jnp.float32),
        in_specs=[
            pl.BlockSpec(memory_space=pltpu.SMEM),
            pl.BlockSpec(memory_space=pltpu.VMEM),
            pl.BlockSpec(memory_space=pltpu.VMEM),
            blk,
            blk,
        ],
        out_specs=pl.BlockSpec(memory_space=pltpu.VMEM),
        scratch_shapes=[
            pltpu.VMEM((width, 2 * half), jnp.bfloat16),
            pltpu.VMEM((2, 2 * half // SUBL, SUBL, LANES), jnp.float32),
            pltpu.VMEM((8, RANKS, SUBL, LANES), jnp.float32),
            pltpu.VMEM((RANKS * SUBL, LANES), jnp.float32),
        ],
        compiler_params=pltpu.CompilerParams(vmem_limit_bytes=48 << 20),
        name="score",
    )(sizes, table, rows, own, peer)


def merge_kernel(idx_ref, r_ref, out_ref, l_ref):
    rows = out_ref.shape[0]
    total = l_ref.shape[0]

    @pl.loop(0, total, unroll=8)
    def _(i):
        l_ref[pl.ds(i, 1), :] = r_ref[pl.ds(idx_ref[i], 1), :]

    lists = l_ref[...]
    while lists.shape[0] > rows:
        h = lists.shape[0] // 2
        lane = lax.broadcasted_iota(jnp.int32, (h, RANKS), 1)
        a, b = lists[:h], lists[h:]
        lists = jnp.maximum(a, jnp.take_along_axis(b, RANKS - 1 - lane, axis=1))
        d = RANKS // 2
        while d:
            other = jnp.take_along_axis(lists, lane ^ d, axis=1)
            lists = jnp.where((lane & d) == 0, jnp.maximum(lists, other), jnp.minimum(lists, other))
            d //= 2
    out_ref[...] = lists[:, : out_ref.shape[1]]


def merge(idx, returned, n_rows):
    total = idx.shape[0]
    return pl.pallas_call(
        merge_kernel,
        out_shape=jax.ShapeDtypeStruct((n_rows, TOPK), jnp.float32),
        in_specs=[pl.BlockSpec(memory_space=pltpu.SMEM), pl.BlockSpec(memory_space=pltpu.VMEM)],
        out_specs=pl.BlockSpec(memory_space=pltpu.VMEM),
        scratch_shapes=[pltpu.VMEM((total, RANKS), jnp.float32)],
        name="merge",
    )(idx, returned)


def local(queries, codebook, probes, codes, part_sizes):
    n_dev = lax.axis_size("dom") * lax.axis_size("sub")
    rep = lax.axis_index("rep")
    own_rows, width = queries.shape
    n_probe = probes.shape[1]
    part_dev, n_groups, half = codes.shape
    n_cent = codebook.shape[1]
    n_parts = part_dev * n_dev
    n_cap = max(2, 2 * own_rows * n_probe // n_parts)
    peer = lax.ppermute(codes, "rep", [(0, 1), (1, 0)])
    send, idx = prep(queries, probes, n_parts * n_cap, n_cap)
    arrived = lax.all_to_all(
        send.reshape(n_dev, part_dev * n_cap, width), ("dom", "sub"), split_axis=0, concat_axis=0, tiled=True
    ).reshape(n_parts * n_cap, width)
    table = jnp.pad(codebook.astype(jnp.float32).transpose(2, 0, 1), ((0, 0), (0, 0), (0, LANES - n_cent)))
    sizes = jnp.stack([part_sizes - rep * half, part_sizes - (1 - rep) * half])
    best = score(sizes, table, arrived, codes, peer, n_cap)
    returned = lax.all_to_all(
        best.reshape(n_dev, part_dev * n_cap, RANKS), ("dom", "sub"), split_axis=0, concat_axis=0, tiled=True
    ).reshape(n_parts * n_cap, RANKS)
    return merge(idx.T.reshape(-1), returned, own_rows)


def solution(mesh):
    in_specs = (
        P(("dom", "sub", "rep"), None),
        P(),
        P(("dom", "sub", "rep"), None),
        P(("dom", "sub"), None, "rep"),
        P(("dom", "sub")),
    )
    out_specs = P(("dom", "sub", "rep"), None)
    return jax.shard_map(local, mesh=mesh, in_specs=in_specs, out_specs=out_specs, check_vma=False)
```

```python
import functools

import jax
import jax.numpy as jnp
from jax import lax
from jax.experimental import pallas as pl
from jax.experimental.pallas import tpu as pltpu
from jax.sharding import PartitionSpec as P

TOPK = 100
MASKED = -1e30
RANKS = 128
LANES = 128
SUBL = 8


def batcher(n):
    pairs = []

    def merge(lo, cnt, r):
        step = r * 2
        if step < cnt:
            merge(lo, cnt, step)
            merge(lo + r, cnt, step)
            for i in range(lo + r, lo + cnt - r, step):
                pairs.append((i, i + r))
        else:
            pairs.append((lo, lo + r))

    def sort(lo, cnt):
        if cnt > 1:
            m = cnt // 2
            sort(lo, m)
            sort(lo + m, m)
            merge(lo, cnt, 1)

    sort(0, n)
    return pairs


SORT32 = batcher(32)


def exchange(x, pairs):
    for i, j in pairs:
        a, b = x[i], x[j]
        x[i] = jnp.maximum(a, b)
        x[j] = jnp.minimum(a, b)
    return x


def clean(x):
    d = len(x) // 2
    while d:
        exchange(x, [(i, i + d) for i in range(len(x)) if not i & d])
        d //= 2
    return x


def prep_kernel(n_cap, q_ref, probes_ref, send_ref, idx_ref):
    rows, width = q_ref.shape
    slots = send_ref.shape[0]
    n = lax.broadcasted_iota(jnp.int32, (rows, slots), 1)
    part = n // n_cap
    rank_of = (n % n_cap).astype(jnp.float32)
    probes = probes_ref[...]
    named = part == probes[:, 0:1]
    for k in range(1, probes.shape[1]):
        named = named | (part == probes[:, k : k + 1])
    before = (
        lax.broadcasted_iota(jnp.int32, (rows, rows), 0) > lax.broadcasted_iota(jnp.int32, (rows, rows), 1)
    ).astype(jnp.float32).astype(jnp.bfloat16)
    rank = jnp.dot(before, named.astype(jnp.float32).astype(jnp.bfloat16), preferred_element_type=jnp.float32)
    chosen = jnp.where(named & (rank == rank_of), 1.0, 0.0)
    nf = n.astype(jnp.float32)
    for k in range(probes.shape[1]):
        hit = jnp.where(part == probes[:, k : k + 1], chosen, 0.0)
        idx_ref[:, k : k + 1] = jnp.sum(hit * nf, axis=1, keepdims=True).astype(jnp.int32)
    a = lax.broadcasted_iota(jnp.int32, (width, width), 0)
    b = lax.broadcasted_iota(jnp.int32, (width, width), 1)
    groups = width // 4
    j = (b >= groups).astype(jnp.int32) + (b >= 2 * groups).astype(jnp.int32) + (b >= 3 * groups).astype(jnp.int32)
    perm = jnp.where(a == (b - groups * j) * 4 + j, 1.0, 0.0).astype(jnp.bfloat16)
    moved = jnp.dot(q_ref[...], perm, preferred_element_type=jnp.float32).astype(jnp.bfloat16)
    picked = lax.dot_general(
        chosen.astype(jnp.bfloat16), moved, (((0,), (0,)), ((), ())), preferred_element_type=jnp.float32
    )
    send_ref[...] = picked.astype(jnp.bfloat16)


def prep(queries, probes, n_slots, n_cap):
    return pl.pallas_call(
        functools.partial(prep_kernel, n_cap),
        out_shape=(
            jax.ShapeDtypeStruct((n_slots, queries.shape[1]), jnp.bfloat16),
            jax.ShapeDtypeStruct(probes.shape, jnp.int32),
        ),
        in_specs=[pl.BlockSpec(memory_space=pltpu.VMEM)] * 2,
        out_specs=[pl.BlockSpec(memory_space=pltpu.VMEM)] * 2,
        compiler_params=pltpu.CompilerParams(vmem_limit_bytes=40 << 20),
        name="prep",
    )(queries, probes)


def sort_block(s_ref, x_ref, b, h):
    groups = s_ref.shape[1] // 32

    @pl.loop(0, groups)
    def _(g):
        x = exchange([s_ref[b, g * 32 + i] for i in range(32)], SORT32)
        for i in range(32):
            s_ref[b, g * 32 + i] = x[i]

    @pl.loop(0, groups // 2)
    def _(g):
        base = g * 64
        low = []
        high = []
        for i in range(32):
            u, v = s_ref[b, base + i], s_ref[b, base + 63 - i]
            high.append(jnp.maximum(u, v))
            low.append(jnp.minimum(u, v))
        clean(high)
        clean(low)
        for i in range(32):
            s_ref[b, base + i] = high[i]
            s_ref[b, base + 32 + i] = low[i]

    @pl.loop(0, groups // 4)
    def _(g):
        base = g * 128

        @pl.loop(0, 32, unroll=8)
        def _(i):
            u0, u1 = s_ref[b, base + i], s_ref[b, base + 32 + i]
            v0, v1 = s_ref[b, base + 127 - i], s_ref[b, base + 95 - i]
            h0, h1 = jnp.maximum(u0, v0), jnp.maximum(u1, v1)
            l0, l1 = jnp.minimum(u0, v0), jnp.minimum(u1, v1)
            x_ref[h, i] = jnp.maximum(h0, h1)
            x_ref[h, 32 + i] = jnp.minimum(h0, h1)
            x_ref[h, 64 + i] = jnp.maximum(l0, l1)
            x_ref[h, 96 + i] = jnp.minimum(l0, l1)

        @pl.loop(0, 4)
        def _(k):
            x = clean([x_ref[h, k * 32 + i] for i in range(32)])
            for i in range(32):
                s_ref[b, base + k * 32 + i] = x[i]

    @pl.loop(0, 32, unroll=8)
    def _(i):
        t = [jnp.maximum(s_ref[b, i + 32 * k], s_ref[b, 255 - i - 32 * k]) for k in range(4)]
        clean(t)
        for k in range(4):
            x_ref[h, i + 32 * k] = t[k]

    @pl.loop(0, 4)
    def _(k):
        x = clean([x_ref[h, k * 32 + i] for i in range(32)])
        for i in range(32):
            x_ref[h, k * 32 + i] = x[i]


def merge_pair(x_ref, b0, b1, level):
    bit = 1 << level
    lower = (lax.broadcasted_iota(jnp.int32, (SUBL, LANES), 0) & bit) == 0

    def joined(i, m):
        first = jnp.where(lower, x_ref[b0, i], x_ref[b1, i])
        second = jnp.where(lower, pltpu.roll(x_ref[b0, m], SUBL - bit, 0), pltpu.roll(x_ref[b1, m], bit, 0))
        return jnp.maximum(first, second)

    @pl.loop(0, 64, unroll=4)
    def _(i):
        m = 127 - i
        s, t = joined(i, m), joined(m, i)
        x_ref[b0, i] = s
        x_ref[b0, m] = t

    @pl.loop(0, 32, unroll=8)
    def _(i):
        t = clean([x_ref[b0, i + 32 * k] for k in range(4)])
        for k in range(4):
            x_ref[b0, i + 32 * k] = t[k]

    @pl.loop(0, 4)
    def _(k):
        x = clean([x_ref[b0, k * 32 + i] for i in range(32)])
        for i in range(32):
            x_ref[b0, k * 32 + i] = x[i]


def decode_kernel(table_ref, codes_ref, d_ref, t_ref):
    groups, half = codes_ref.shape[1:]

    @pl.loop(0, groups // 16)
    def _(g):
        rows = pl.ds(pl.multiple_of(g * 16, 16), 16)
        tab = [table_ref[j, rows, :] for j in range(4)]
        for t in range(half // LANES):
            cols = slice(t * LANES, (t + 1) * LANES)
            c = codes_ref[0, rows, cols]
            for j in range(4):
                val = jnp.take_along_axis(tab[j], c, axis=1)
                t_ref[pl.ds(pl.multiple_of(j * groups + g * 16, 16), 16), cols] = val.astype(jnp.bfloat16)

    @pl.loop(0, half // 256)
    def _(t):
        cols = pl.ds(pl.multiple_of(t * 256, 256), 256)
        d_ref[0, cols, :] = t_ref[:, cols].T


def decode(table, codes):
    part_dev, groups, half = codes.shape
    width = groups * 4
    return pl.pallas_call(
        decode_kernel,
        grid=(part_dev,),
        out_shape=jax.ShapeDtypeStruct((part_dev, half, width), jnp.bfloat16),
        in_specs=[
            pl.BlockSpec(memory_space=pltpu.VMEM),
            pl.BlockSpec((1, groups, half), lambda p: (p, 0, 0)),
        ],
        out_specs=pl.BlockSpec((1, half, width), lambda p: (p, 0, 0)),
        scratch_shapes=[pltpu.VMEM((width, half), jnp.bfloat16)],
        compiler_params=pltpu.CompilerParams(vmem_limit_bytes=56 << 20),
        cost_estimate=pl.CostEstimate(flops=10**10, bytes_accessed=20 << 20, transcendentals=0),
        name="decode",
    )(table, codes)


def score_kernel(n_cap, sizes_ref, q_ref, own_ref, peer_ref, out_ref, s_ref, x_ref, z_ref):
    p = pl.program_id(0)
    half = own_ref.shape[1]
    part_dev = pl.num_programs(0)

    all_rows = q_ref.shape[0]
    m = lax.broadcasted_iota(jnp.int32, (256, all_rows), 0)
    src = (m // 128) * 32 + m % 32
    want = src * (part_dev * n_cap) + p * n_cap + (m % 128) // 32
    pick = jnp.where(lax.broadcasted_iota(jnp.int32, (256, all_rows), 1) == want, 1.0, 0.0).astype(jnp.bfloat16)
    mine = jnp.dot(pick, q_ref[...], preferred_element_type=jnp.float32).astype(jnp.bfloat16)

    for which, ref in enumerate((own_ref, peer_ref)):
        sc = lax.dot_general(ref[0], mine, (((1,), (1,)), ((), ())), preferred_element_type=jnp.float32)
        ok = lax.broadcasted_iota(jnp.int32, (half, LANES), 0) < sizes_ref[which, p]
        for h in range(2):
            blk = jnp.where(ok, sc[:, h * LANES : (h + 1) * LANES], MASKED)
            s_ref[h, pl.ds(which * half // SUBL, half // SUBL)] = blk.reshape(half // SUBL, SUBL, LANES)

    for h in range(2):
        sort_block(s_ref, x_ref, h, p * 2 + h)

    @pl.when(p == part_dev - 1)
    def _():
        for b in range(0, 8, 2):
            merge_pair(x_ref, b, b + 1, 2)
        for b in range(0, 8, 4):
            merge_pair(x_ref, b, b + 2, 1)
        merge_pair(x_ref, 0, 4, 0)
        z_ref[...] = x_ref[0].reshape(RANKS * SUBL, LANES)
        for blk in range(8):
            u = 4 * (blk & 1) + (blk & 2) + (blk >> 2)
            got = z_ref[pl.ds(u, RANKS, stride=SUBL), :].T
            for r in range(n_cap):
                base = (blk & 1) * 32 * 16 + (blk >> 1) * n_cap + r
                out_ref[pl.ds(base, 32, stride=16), :] = got[r * 32 : (r + 1) * 32, :]


def score(sizes, rows, own, peer, n_cap):
    part_dev, half, width = own.shape
    n_rows = rows.shape[0]
    blk = pl.BlockSpec((1, half, width), lambda p: (p, 0, 0))
    return pl.pallas_call(
        functools.partial(score_kernel, n_cap),
        grid=(part_dev,),
        out_shape=jax.ShapeDtypeStruct((n_rows, RANKS), jnp.float32),
        in_specs=[
            pl.BlockSpec(memory_space=pltpu.SMEM),
            pl.BlockSpec(memory_space=pltpu.VMEM),
            blk,
            blk,
        ],
        out_specs=pl.BlockSpec(memory_space=pltpu.VMEM),
        scratch_shapes=[
            pltpu.VMEM((2, 2 * half // SUBL, SUBL, LANES), jnp.float32),
            pltpu.VMEM((8, RANKS, SUBL, LANES), jnp.float32),
            pltpu.VMEM((RANKS * SUBL, LANES), jnp.float32),
        ],
        compiler_params=pltpu.CompilerParams(vmem_limit_bytes=40 << 20),
        name="score",
    )(sizes, rows, own, peer)


def merge_kernel(idx_ref, r_ref, out_ref, l_ref):
    rows = out_ref.shape[0]
    total = l_ref.shape[0]

    @pl.loop(0, total, unroll=8)
    def _(i):
        l_ref[pl.ds(i, 1), :] = r_ref[pl.ds(idx_ref[i], 1), :]

    lists = l_ref[...]
    while lists.shape[0] > rows:
        h = lists.shape[0] // 2
        lane = lax.broadcasted_iota(jnp.int32, (h, RANKS), 1)
        a, b = lists[:h], lists[h:]
        lists = jnp.maximum(a, jnp.take_along_axis(b, RANKS - 1 - lane, axis=1))
        d = RANKS // 2
        while d:
            other = jnp.take_along_axis(lists, lane ^ d, axis=1)
            lists = jnp.where((lane & d) == 0, jnp.maximum(lists, other), jnp.minimum(lists, other))
            d //= 2
    out_ref[...] = lists[:, : out_ref.shape[1]]


def merge(idx, returned, n_rows):
    total = idx.shape[0]
    return pl.pallas_call(
        merge_kernel,
        out_shape=jax.ShapeDtypeStruct((n_rows, TOPK), jnp.float32),
        in_specs=[pl.BlockSpec(memory_space=pltpu.SMEM), pl.BlockSpec(memory_space=pltpu.VMEM)],
        out_specs=pl.BlockSpec(memory_space=pltpu.VMEM),
        scratch_shapes=[pltpu.VMEM((total, RANKS), jnp.float32)],
        compiler_params=pltpu.CompilerParams(vmem_limit_bytes=16 << 20),
        name="merge",
    )(idx, returned)


def local(queries, codebook, probes, codes, part_sizes):
    n_dev = lax.axis_size("dom") * lax.axis_size("sub")
    rep = lax.axis_index("rep")
    own_rows, width = queries.shape
    n_probe = probes.shape[1]
    part_dev, n_groups, half = codes.shape
    n_cent = codebook.shape[1]
    n_parts = part_dev * n_dev
    n_cap = max(2, 2 * own_rows * n_probe // n_parts)
    peer = lax.ppermute(codes, "rep", [(0, 1), (1, 0)])
    send, idx = prep(queries, probes, n_parts * n_cap, n_cap)
    arrived = lax.all_to_all(
        send.reshape(n_dev, part_dev * n_cap, width), ("dom", "sub"), split_axis=0, concat_axis=0, tiled=True
    ).reshape(n_parts * n_cap, width)
    table = jnp.pad(codebook.astype(jnp.float32).transpose(2, 0, 1), ((0, 0), (0, 0), (0, LANES - n_cent)))
    sizes = jnp.stack([part_sizes - rep * half, part_sizes - (1 - rep) * half])
    best = score(sizes, arrived, decode(table, codes), decode(table, peer), n_cap)
    returned = lax.all_to_all(
        best.reshape(n_dev, part_dev * n_cap, RANKS), ("dom", "sub"), split_axis=0, concat_axis=0, tiled=True
    ).reshape(n_parts * n_cap, RANKS)
    return merge(idx.T.reshape(-1), returned, own_rows)


def solution(mesh):
    in_specs = (
        P(("dom", "sub", "rep"), None),
        P(),
        P(("dom", "sub", "rep"), None),
        P(("dom", "sub"), None, "rep"),
        P(("dom", "sub")),
    )
    out_specs = P(("dom", "sub", "rep"), None)
    return jax.shard_map(local, mesh=mesh, in_specs=in_specs, out_specs=out_specs, check_vma=False)
```

```python
import functools

import jax
import jax.numpy as jnp
from jax import lax
from jax.experimental import pallas as pl
from jax.experimental.pallas import tpu as pltpu
from jax.sharding import PartitionSpec as P

TOPK = 100
MASKED = -1e30
RANKS = 128
LANES = 128
SUBL = 8


def batcher(n):
    pairs = []

    def merge(lo, cnt, r):
        step = r * 2
        if step < cnt:
            merge(lo, cnt, step)
            merge(lo + r, cnt, step)
            for i in range(lo + r, lo + cnt - r, step):
                pairs.append((i, i + r))
        else:
            pairs.append((lo, lo + r))

    def sort(lo, cnt):
        if cnt > 1:
            m = cnt // 2
            sort(lo, m)
            sort(lo + m, m)
            merge(lo, cnt, 1)

    sort(0, n)
    return pairs


SORT32 = batcher(32)


def exchange(x, pairs):
    for i, j in pairs:
        a, b = x[i], x[j]
        x[i] = jnp.maximum(a, b)
        x[j] = jnp.minimum(a, b)
    return x


def clean(x):
    d = len(x) // 2
    while d:
        exchange(x, [(i, i + d) for i in range(len(x)) if not i & d])
        d //= 2
    return x


MESH = pl.DeviceIdType.MESH


def device_of(t):
    n_sub = lax.axis_size("sub")
    return {"dom": t // n_sub, "sub": t % n_sub}


def route(n_cap, q_ref, probes_ref, send_ref, idx_ref):
    rows, width = q_ref.shape
    n_dev, chip_slots, _ = send_ref.shape
    slots = n_dev * chip_slots
    n = lax.broadcasted_iota(jnp.int32, (rows, slots), 1)
    part = n // n_cap
    rank_of = (n % n_cap).astype(jnp.float32)
    probes = probes_ref[...]
    named = part == probes[:, 0:1]
    for k in range(1, probes.shape[1]):
        named = named | (part == probes[:, k : k + 1])
    before = (
        lax.broadcasted_iota(jnp.int32, (rows, rows), 0) > lax.broadcasted_iota(jnp.int32, (rows, rows), 1)
    ).astype(jnp.float32).astype(jnp.bfloat16)
    rank = jnp.dot(before, named.astype(jnp.float32).astype(jnp.bfloat16), preferred_element_type=jnp.float32)
    chosen = jnp.where(named & (rank == rank_of), 1.0, 0.0)
    nf = n.astype(jnp.float32)
    for k in range(probes.shape[1]):
        hit = jnp.where(part == probes[:, k : k + 1], chosen, 0.0)
        idx_ref[:, k : k + 1] = jnp.sum(hit * nf, axis=1, keepdims=True).astype(jnp.int32)
    a = lax.broadcasted_iota(jnp.int32, (width, width), 0)
    b = lax.broadcasted_iota(jnp.int32, (width, width), 1)
    groups = width // 4
    j = (b >= groups).astype(jnp.int32) + (b >= 2 * groups).astype(jnp.int32) + (b >= 3 * groups).astype(jnp.int32)
    perm = jnp.where(a == (b - groups * j) * 4 + j, 1.0, 0.0).astype(jnp.bfloat16)
    moved = jnp.dot(q_ref[...], perm, preferred_element_type=jnp.float32).astype(jnp.bfloat16)
    picked = lax.dot_general(
        chosen.astype(jnp.bfloat16), moved, (((0,), (0,)), ((), ())), preferred_element_type=jnp.float32
    )
    send_ref[...] = picked.astype(jnp.bfloat16).reshape(send_ref.shape)


def decode(table_ref, codes_ref, p, t_ref, d_ref, slot):
    groups, half = codes_ref.shape[1:]

    @pl.loop(0, groups // 16)
    def _(g):
        rows = pl.ds(pl.multiple_of(g * 16, 16), 16)
        tab = [table_ref[j, rows, :] for j in range(4)]
        for t in range(half // LANES):
            cols = slice(t * LANES, (t + 1) * LANES)
            c = codes_ref[p, rows, cols]
            for j in range(4):
                val = jnp.take_along_axis(tab[j], c, axis=1)
                t_ref[pl.ds(pl.multiple_of(j * groups + g * 16, 16), 16), cols] = val.astype(jnp.bfloat16)

    @pl.loop(0, half // 256)
    def _(t):
        cols = pl.ds(pl.multiple_of(t * 256, 256), 256)
        d_ref[slot, cols, :] = t_ref[:, cols].T


def fetch_kernel(
    n_cap, q_ref, probes_ref, table_ref, codes_ref, rows_ref, idx_ref, d_out,
    send_ref, own_ref, peer_ref, t_ref, d_ref,
    in_sem, out_sem, code_send, code_recv, row_send, row_recv, local_sem,
):
    n_dev = send_ref.shape[0]
    part_dev = codes_ref.shape[0]
    me = lax.axis_index("dom") * lax.axis_size("sub") + lax.axis_index("sub")
    other = {"rep": 1 - lax.axis_index("rep")}

    loads = [pltpu.make_async_copy(codes_ref.at[p], own_ref.at[p], in_sem.at[p]) for p in range(part_dev)]
    for c in loads:
        c.start()
    barrier = pltpu.get_barrier_semaphore()
    pl.semaphore_signal(barrier, inc=1, device_id=other, device_id_type=MESH)

    @pl.loop(1, n_dev)
    def _(k):
        pl.semaphore_signal(barrier, inc=1, device_id=device_of((me + k) % n_dev), device_id_type=MESH)

    route(n_cap, q_ref, probes_ref, send_ref, idx_ref)
    pl.semaphore_wait(barrier, n_dev)

    def row_copy(k):
        t = (me + k) % n_dev
        return pltpu.make_async_remote_copy(
            src_ref=send_ref.at[t],
            dst_ref=rows_ref.at[me],
            send_sem=row_send.at[k],
            recv_sem=row_recv.at[k],
            device_id=device_of(t),
            device_id_type=MESH,
        )

    @pl.loop(1, n_dev)
    def _(k):
        row_copy(k).start()

    swaps = [
        pltpu.make_async_remote_copy(
            src_ref=codes_ref.at[p],
            dst_ref=peer_ref.at[p],
            send_sem=code_send.at[p],
            recv_sem=code_recv.at[p],
            device_id=other,
            device_id_type=MESH,
        )
        for p in range(part_dev)
    ]
    for c in swaps:
        c.start()
    keep = pltpu.make_async_copy(send_ref.at[me], rows_ref.at[me], local_sem)
    keep.start()

    writes = []
    for which, ref in enumerate((own_ref, peer_ref)):
        for p in range(part_dev):
            n = which * part_dev + p
            if which == 0:
                loads[p].wait()
            else:
                swaps[p].wait()
            if n >= 2:
                writes[n - 2].wait()
            decode(table_ref, ref, p, t_ref, d_ref, n % 2)
            w = pltpu.make_async_copy(d_ref.at[n % 2], d_out.at[which, p], out_sem.at[n])
            w.start()
            writes.append(w)
    keep.wait()

    @pl.loop(1, n_dev)
    def _(k):
        row_copy(k).wait()

    writes[-2].wait()
    writes[-1].wait()


def fetch(queries, probes, table, codes, n_dev, n_cap):
    part_dev, groups, half = codes.shape
    width = queries.shape[1]
    vmem = pl.BlockSpec(memory_space=pltpu.VMEM)
    hbm = pl.BlockSpec(memory_space=pl.ANY)
    dma = pltpu.SemaphoreType.DMA
    return pl.pallas_call(
        functools.partial(fetch_kernel, n_cap),
        out_shape=(
            jax.ShapeDtypeStruct((n_dev, part_dev * n_cap, width), jnp.bfloat16),
            jax.ShapeDtypeStruct(probes.shape, jnp.int32),
            jax.ShapeDtypeStruct((2, part_dev, half, width), jnp.bfloat16),
        ),
        in_specs=[vmem, vmem, vmem, hbm],
        out_specs=[hbm, vmem, hbm],
        scratch_shapes=[
            pltpu.VMEM((n_dev, part_dev * n_cap, width), jnp.bfloat16),
            pltpu.VMEM(codes.shape, jnp.int32),
            pltpu.VMEM(codes.shape, jnp.int32),
            pltpu.VMEM((width, half), jnp.bfloat16),
            pltpu.VMEM((2, half, width), jnp.bfloat16),
            dma((part_dev,)),
            dma((2 * part_dev,)),
            dma((part_dev,)),
            dma((part_dev,)),
            dma((n_dev,)),
            dma((n_dev,)),
            dma,
        ],
        compiler_params=pltpu.CompilerParams(collective_id=0, has_side_effects=True, vmem_limit_bytes=56 << 20),
        name="fetch",
    )(queries, probes, table, codes)


def sort_block(s_ref, x_ref, b, h):
    groups = s_ref.shape[1] // 32

    @pl.loop(0, groups)
    def _(g):
        x = exchange([s_ref[b, g * 32 + i] for i in range(32)], SORT32)
        for i in range(32):
            s_ref[b, g * 32 + i] = x[i]

    @pl.loop(0, groups // 2)
    def _(g):
        base = g * 64
        low = []
        high = []
        for i in range(32):
            u, v = s_ref[b, base + i], s_ref[b, base + 63 - i]
            high.append(jnp.maximum(u, v))
            low.append(jnp.minimum(u, v))
        clean(high)
        clean(low)
        for i in range(32):
            s_ref[b, base + i] = high[i]
            s_ref[b, base + 32 + i] = low[i]

    @pl.loop(0, groups // 4)
    def _(g):
        base = g * 128

        @pl.loop(0, 32, unroll=8)
        def _(i):
            u0, u1 = s_ref[b, base + i], s_ref[b, base + 32 + i]
            v0, v1 = s_ref[b, base + 127 - i], s_ref[b, base + 95 - i]
            h0, h1 = jnp.maximum(u0, v0), jnp.maximum(u1, v1)
            l0, l1 = jnp.minimum(u0, v0), jnp.minimum(u1, v1)
            x_ref[h, i] = jnp.maximum(h0, h1)
            x_ref[h, 32 + i] = jnp.minimum(h0, h1)
            x_ref[h, 64 + i] = jnp.maximum(l0, l1)
            x_ref[h, 96 + i] = jnp.minimum(l0, l1)

        @pl.loop(0, 4)
        def _(k):
            x = clean([x_ref[h, k * 32 + i] for i in range(32)])
            for i in range(32):
                s_ref[b, base + k * 32 + i] = x[i]

    @pl.loop(0, 32, unroll=8)
    def _(i):
        t = [jnp.maximum(s_ref[b, i + 32 * k], s_ref[b, 255 - i - 32 * k]) for k in range(4)]
        clean(t)
        for k in range(4):
            x_ref[h, i + 32 * k] = t[k]

    @pl.loop(0, 4)
    def _(k):
        x = clean([x_ref[h, k * 32 + i] for i in range(32)])
        for i in range(32):
            x_ref[h, k * 32 + i] = x[i]


def merge_pair(x_ref, b0, b1, level):
    bit = 1 << level
    lower = (lax.broadcasted_iota(jnp.int32, (SUBL, LANES), 0) & bit) == 0

    def joined(i, m):
        first = jnp.where(lower, x_ref[b0, i], x_ref[b1, i])
        second = jnp.where(lower, pltpu.roll(x_ref[b0, m], SUBL - bit, 0), pltpu.roll(x_ref[b1, m], bit, 0))
        return jnp.maximum(first, second)

    @pl.loop(0, 64, unroll=4)
    def _(i):
        m = 127 - i
        s, t = joined(i, m), joined(m, i)
        x_ref[b0, i] = s
        x_ref[b0, m] = t

    @pl.loop(0, 32, unroll=8)
    def _(i):
        t = clean([x_ref[b0, i + 32 * k] for k in range(4)])
        for k in range(4):
            x_ref[b0, i + 32 * k] = t[k]

    @pl.loop(0, 4)
    def _(k):
        x = clean([x_ref[b0, k * 32 + i] for i in range(32)])
        for i in range(32):
            x_ref[b0, k * 32 + i] = x[i]


def score_kernel(n_cap, sizes_ref, q_ref, own_ref, peer_ref, out_ref, s_ref, x_ref, z_ref):
    p = pl.program_id(0)
    half = own_ref.shape[2]
    part_dev = pl.num_programs(0)

    all_rows = q_ref.shape[0]
    m = lax.broadcasted_iota(jnp.int32, (256, all_rows), 0)
    src = (m // 128) * 32 + m % 32
    want = src * (part_dev * n_cap) + p * n_cap + (m % 128) // 32
    pick = jnp.where(lax.broadcasted_iota(jnp.int32, (256, all_rows), 1) == want, 1.0, 0.0).astype(jnp.bfloat16)
    mine = jnp.dot(pick, q_ref[...], preferred_element_type=jnp.float32).astype(jnp.bfloat16)

    for which, ref in enumerate((own_ref, peer_ref)):
        sc = lax.dot_general(ref[0, 0], mine, (((1,), (1,)), ((), ())), preferred_element_type=jnp.float32)
        ok = lax.broadcasted_iota(jnp.int32, (half, LANES), 0) < sizes_ref[which, p]
        for h in range(2):
            blk = jnp.where(ok, sc[:, h * LANES : (h + 1) * LANES], MASKED)
            s_ref[h, pl.ds(which * half // SUBL, half // SUBL)] = blk.reshape(half // SUBL, SUBL, LANES)

    for h in range(2):
        sort_block(s_ref, x_ref, h, p * 2 + h)

    @pl.when(p == part_dev - 1)
    def _():
        for b in range(0, 8, 2):
            merge_pair(x_ref, b, b + 1, 2)
        for b in range(0, 8, 4):
            merge_pair(x_ref, b, b + 2, 1)
        merge_pair(x_ref, 0, 4, 0)
        z_ref[...] = x_ref[0].reshape(RANKS * SUBL, LANES)
        for blk in range(8):
            u = 4 * (blk & 1) + (blk & 2) + (blk >> 2)
            got = z_ref[pl.ds(u, RANKS, stride=SUBL), :].T
            for r in range(n_cap):
                base = (blk & 1) * 32 * 16 + (blk >> 1) * n_cap + r
                out_ref[pl.ds(base, 32, stride=16), :] = got[r * 32 : (r + 1) * 32, :]


def score(sizes, rows, decoded, n_cap):
    _, part_dev, half, width = decoded.shape
    n_rows = rows.shape[0]
    return pl.pallas_call(
        functools.partial(score_kernel, n_cap),
        grid=(part_dev,),
        out_shape=jax.ShapeDtypeStruct((n_rows, RANKS), jnp.float32),
        in_specs=[
            pl.BlockSpec(memory_space=pltpu.SMEM),
            pl.BlockSpec(memory_space=pltpu.VMEM),
            pl.BlockSpec((1, 1, half, width), lambda p: (0, p, 0, 0)),
            pl.BlockSpec((1, 1, half, width), lambda p: (1, p, 0, 0)),
        ],
        out_specs=pl.BlockSpec(memory_space=pltpu.VMEM),
        scratch_shapes=[
            pltpu.VMEM((2, 2 * half // SUBL, SUBL, LANES), jnp.float32),
            pltpu.VMEM((8, RANKS, SUBL, LANES), jnp.float32),
            pltpu.VMEM((RANKS * SUBL, LANES), jnp.float32),
        ],
        compiler_params=pltpu.CompilerParams(vmem_limit_bytes=46 << 20),
        name="score",
    )(sizes, rows, decoded, decoded)


def merge_kernel(idx_ref, r_ref, out_ref, l_ref):
    rows = out_ref.shape[0]
    total = l_ref.shape[0]

    @pl.loop(0, total, unroll=8)
    def _(i):
        l_ref[pl.ds(i, 1), :] = r_ref[pl.ds(idx_ref[i], 1), :]

    lists = l_ref[...]
    while lists.shape[0] > rows:
        h = lists.shape[0] // 2
        lane = lax.broadcasted_iota(jnp.int32, (h, RANKS), 1)
        a, b = lists[:h], lists[h:]
        lists = jnp.maximum(a, jnp.take_along_axis(b, RANKS - 1 - lane, axis=1))
        d = RANKS // 2
        while d:
            other = jnp.take_along_axis(lists, lane ^ d, axis=1)
            lists = jnp.where((lane & d) == 0, jnp.maximum(lists, other), jnp.minimum(lists, other))
            d //= 2
    out_ref[...] = lists[:, : out_ref.shape[1]]


def merge(idx, returned, n_rows):
    total = idx.shape[0]
    return pl.pallas_call(
        merge_kernel,
        out_shape=jax.ShapeDtypeStruct((n_rows, TOPK), jnp.float32),
        in_specs=[pl.BlockSpec(memory_space=pltpu.SMEM), pl.BlockSpec(memory_space=pltpu.VMEM)],
        out_specs=pl.BlockSpec(memory_space=pltpu.VMEM),
        scratch_shapes=[pltpu.VMEM((total, RANKS), jnp.float32)],
        compiler_params=pltpu.CompilerParams(vmem_limit_bytes=16 << 20),
        name="merge",
    )(idx, returned)


def local(queries, codebook, probes, codes, part_sizes):
    n_dev = lax.axis_size("dom") * lax.axis_size("sub")
    rep = lax.axis_index("rep")
    own_rows, width = queries.shape
    n_probe = probes.shape[1]
    part_dev, n_groups, half = codes.shape
    n_cent = codebook.shape[1]
    n_parts = part_dev * n_dev
    n_cap = max(2, 2 * own_rows * n_probe // n_parts)
    table = jnp.pad(codebook.astype(jnp.float32).transpose(2, 0, 1), ((0, 0), (0, 0), (0, LANES - n_cent)))
    sizes = jnp.stack([part_sizes - rep * half, part_sizes - (1 - rep) * half])
    arrived, idx, decoded = fetch(queries, probes, table, codes, n_dev, n_cap)
    best = score(sizes, arrived.reshape(n_parts * n_cap, width), decoded, n_cap)
    returned = lax.all_to_all(
        best.reshape(n_dev, part_dev * n_cap, RANKS), ("dom", "sub"), split_axis=0, concat_axis=0, tiled=True
    ).reshape(n_parts * n_cap, RANKS)
    return merge(idx.T.reshape(-1), returned, own_rows)


def solution(mesh):
    in_specs = (
        P(("dom", "sub", "rep"), None),
        P(),
        P(("dom", "sub", "rep"), None),
        P(("dom", "sub"), None, "rep"),
        P(("dom", "sub")),
    )
    out_specs = P(("dom", "sub", "rep"), None)
    return jax.shard_map(local, mesh=mesh, in_specs=in_specs, out_specs=out_specs, check_vma=False)
```

```python
import functools

import jax
import jax.numpy as jnp
from jax import lax
from jax.experimental import pallas as pl
from jax.experimental.pallas import tpu as pltpu
from jax.sharding import PartitionSpec as P

TOPK = 100
MASKED = -1e30
RANKS = 128
LANES = 128
SUBL = 8


def batcher(n):
    pairs = []

    def merge(lo, cnt, r):
        step = r * 2
        if step < cnt:
            merge(lo, cnt, step)
            merge(lo + r, cnt, step)
            for i in range(lo + r, lo + cnt - r, step):
                pairs.append((i, i + r))
        else:
            pairs.append((lo, lo + r))

    def sort(lo, cnt):
        if cnt > 1:
            m = cnt // 2
            sort(lo, m)
            sort(lo + m, m)
            merge(lo, cnt, 1)

    sort(0, n)
    return pairs


SORT32 = batcher(32)


def exchange(x, pairs):
    for i, j in pairs:
        a, b = x[i], x[j]
        x[i] = jnp.maximum(a, b)
        x[j] = jnp.minimum(a, b)
    return x


def clean(x):
    d = len(x) // 2
    while d:
        exchange(x, [(i, i + d) for i in range(len(x)) if not i & d])
        d //= 2
    return x


MESH = pl.DeviceIdType.MESH


def device_of(t):
    n_sub = lax.axis_size("sub")
    return {"dom": t // n_sub, "sub": t % n_sub}


def route(n_cap, q_ref, probes_ref, send_ref, idx_ref):
    rows, width = q_ref.shape
    n_dev, chip_slots, _ = send_ref.shape
    slots = n_dev * chip_slots
    n = lax.broadcasted_iota(jnp.int32, (slots, rows), 0)
    part = n // n_cap
    rank_of = (n % n_cap).astype(jnp.float32)
    n_probe = probes_ref.shape[0]
    hits = [part == probes_ref[k : k + 1, :] for k in range(n_probe)]
    named = hits[0]
    for k in range(1, n_probe):
        named = named | hits[k]
    before = (
        lax.broadcasted_iota(jnp.int32, (rows, rows), 0) < lax.broadcasted_iota(jnp.int32, (rows, rows), 1)
    ).astype(jnp.float32).astype(jnp.bfloat16)
    rank = jnp.dot(named.astype(jnp.float32).astype(jnp.bfloat16), before, preferred_element_type=jnp.float32)
    chosen = named & (rank == rank_of)
    nf = jnp.where(chosen, n, 0)
    for k in range(n_probe):
        idx_ref[k : k + 1, :] = jnp.sum(jnp.where(hits[k], nf, 0), axis=0, keepdims=True)
    a = lax.broadcasted_iota(jnp.int32, (width, width), 0)
    b = lax.broadcasted_iota(jnp.int32, (width, width), 1)
    groups = width // 4
    j = (b >= groups).astype(jnp.int32) + (b >= 2 * groups).astype(jnp.int32) + (b >= 3 * groups).astype(jnp.int32)
    perm = jnp.where(a == (b - groups * j) * 4 + j, 1.0, 0.0).astype(jnp.bfloat16)
    moved = jnp.dot(q_ref[...], perm, preferred_element_type=jnp.float32).astype(jnp.bfloat16)
    pick = jnp.where(chosen, 1.0, 0.0).astype(jnp.bfloat16)
    picked = jnp.dot(pick, moved, preferred_element_type=jnp.float32)
    send_ref[...] = picked.astype(jnp.bfloat16).reshape(send_ref.shape)


def fill_table(book_ref, table_ref):
    n_cent, n_feat, groups = book_ref.shape
    for j in range(n_feat):
        plane = book_ref[:, j, :].astype(jnp.float32)
        wide = jnp.concatenate([plane, jnp.zeros((LANES - n_cent, groups), jnp.float32)], axis=0)
        table_ref[j] = wide.T


def decode(table_ref, codes_ref, p, t_ref, d_ref, slot):
    groups, half = codes_ref.shape[1:]

    @pl.loop(0, groups // 16)
    def _(g):
        rows = pl.ds(pl.multiple_of(g * 16, 16), 16)
        tab = [table_ref[j, rows, :] for j in range(4)]
        for t in range(half // LANES):
            cols = slice(t * LANES, (t + 1) * LANES)
            c = codes_ref[p, rows, cols]
            for j in range(4):
                val = jnp.take_along_axis(tab[j], c, axis=1)
                t_ref[pl.ds(pl.multiple_of(j * groups + g * 16, 16), 16), cols] = val.astype(jnp.bfloat16)

    @pl.loop(0, half // 256)
    def _(t):
        cols = pl.ds(pl.multiple_of(t * 256, 256), 256)
        d_ref[slot, cols, :] = t_ref[:, cols].T


def fetch_kernel(
    n_cap, q_ref, probes_ref, book_ref, codes_ref, rows_ref, idx_ref, d_out,
    send_ref, own_ref, peer_ref, t_ref, d_ref, table_ref,
    in_sem, out_sem, code_send, code_recv, row_send, row_recv, local_sem,
):
    n_dev = send_ref.shape[0]
    part_dev = codes_ref.shape[0]
    me = lax.axis_index("dom") * lax.axis_size("sub") + lax.axis_index("sub")
    other = {"rep": 1 - lax.axis_index("rep")}

    loads = [pltpu.make_async_copy(codes_ref.at[p], own_ref.at[p], in_sem.at[p]) for p in range(part_dev)]
    for c in loads:
        c.start()
    barrier = pltpu.get_barrier_semaphore()
    pl.semaphore_signal(barrier, inc=1, device_id=other, device_id_type=MESH)

    @pl.loop(1, n_dev)
    def _(k):
        pl.semaphore_signal(barrier, inc=1, device_id=device_of((me + k) % n_dev), device_id_type=MESH)

    route(n_cap, q_ref, probes_ref, send_ref, idx_ref)
    pl.semaphore_wait(barrier, n_dev)

    def row_copy(k):
        t = (me + k) % n_dev
        return pltpu.make_async_remote_copy(
            src_ref=send_ref.at[t],
            dst_ref=rows_ref.at[me],
            send_sem=row_send.at[k],
            recv_sem=row_recv.at[k],
            device_id=device_of(t),
            device_id_type=MESH,
        )

    @pl.loop(1, n_dev)
    def _(k):
        row_copy(k).start()

    swaps = [
        pltpu.make_async_remote_copy(
            src_ref=codes_ref.at[p],
            dst_ref=peer_ref.at[p],
            send_sem=code_send.at[p],
            recv_sem=code_recv.at[p],
            device_id=other,
            device_id_type=MESH,
        )
        for p in range(part_dev)
    ]
    for c in swaps:
        c.start()
    keep = pltpu.make_async_copy(send_ref.at[me], rows_ref.at[me], local_sem)
    keep.start()
    fill_table(book_ref, table_ref)

    writes = []
    for which, ref in enumerate((own_ref, peer_ref)):
        for p in range(part_dev):
            n = which * part_dev + p
            if which == 0:
                loads[p].wait()
            else:
                swaps[p].wait()
            if n >= 2:
                writes[n - 2].wait()
            decode(table_ref, ref, p, t_ref, d_ref, n % 2)
            w = pltpu.make_async_copy(d_ref.at[n % 2], d_out.at[which, p], out_sem.at[n])
            w.start()
            writes.append(w)
    keep.wait()

    @pl.loop(1, n_dev)
    def _(k):
        row_copy(k).wait()

    writes[-2].wait()
    writes[-1].wait()


def fetch(queries, probes, book, codes, n_dev, n_cap):
    part_dev, groups, half = codes.shape
    width = queries.shape[1]
    vmem = pl.BlockSpec(memory_space=pltpu.VMEM)
    hbm = pl.BlockSpec(memory_space=pl.ANY)
    dma = pltpu.SemaphoreType.DMA
    return pl.pallas_call(
        functools.partial(fetch_kernel, n_cap),
        out_shape=(
            jax.ShapeDtypeStruct((n_dev, part_dev * n_cap, width), jnp.bfloat16),
            jax.ShapeDtypeStruct(probes.shape, jnp.int32),
            jax.ShapeDtypeStruct((2, part_dev, half, width), jnp.bfloat16),
        ),
        in_specs=[vmem, vmem, vmem, pl.BlockSpec(memory_space=pltpu.HBM)],
        out_specs=[hbm, vmem, hbm],
        scratch_shapes=[
            pltpu.VMEM((n_dev, part_dev * n_cap, width), jnp.bfloat16),
            pltpu.VMEM(codes.shape, jnp.int32),
            pltpu.VMEM(codes.shape, jnp.int32),
            pltpu.VMEM((width, half), jnp.bfloat16),
            pltpu.VMEM((2, half, width), jnp.bfloat16),
            pltpu.VMEM((book.shape[1], groups, LANES), jnp.float32),
            dma((part_dev,)),
            dma((2 * part_dev,)),
            dma((part_dev,)),
            dma((part_dev,)),
            dma((n_dev,)),
            dma((n_dev,)),
            dma,
        ],
        compiler_params=pltpu.CompilerParams(collective_id=0, has_side_effects=True, vmem_limit_bytes=22 << 20),
        name="fetch",
    )(queries, probes, book, codes)


def sort_block(s_ref, x_ref, b, h):
    groups = s_ref.shape[1] // 32

    @pl.loop(0, groups)
    def _(g):
        x = exchange([s_ref[b, g * 32 + i] for i in range(32)], SORT32)
        for i in range(32):
            s_ref[b, g * 32 + i] = x[i]

    @pl.loop(0, groups // 2)
    def _(g):
        base = g * 64
        low = []
        high = []
        for i in range(32):
            u, v = s_ref[b, base + i], s_ref[b, base + 63 - i]
            high.append(jnp.maximum(u, v))
            low.append(jnp.minimum(u, v))
        clean(high)
        clean(low)
        for i in range(32):
            s_ref[b, base + i] = high[i]
            s_ref[b, base + 32 + i] = low[i]

    @pl.loop(0, groups // 4)
    def _(g):
        base = g * 128

        @pl.loop(0, 32, unroll=8)
        def _(i):
            u0, u1 = s_ref[b, base + i], s_ref[b, base + 32 + i]
            v0, v1 = s_ref[b, base + 127 - i], s_ref[b, base + 95 - i]
            h0, h1 = jnp.maximum(u0, v0), jnp.maximum(u1, v1)
            l0, l1 = jnp.minimum(u0, v0), jnp.minimum(u1, v1)
            x_ref[h, i] = jnp.maximum(h0, h1)
            x_ref[h, 32 + i] = jnp.minimum(h0, h1)
            x_ref[h, 64 + i] = jnp.maximum(l0, l1)
            x_ref[h, 96 + i] = jnp.minimum(l0, l1)

        @pl.loop(0, 4)
        def _(k):
            x = clean([x_ref[h, k * 32 + i] for i in range(32)])
            for i in range(32):
                s_ref[b, base + k * 32 + i] = x[i]

    @pl.loop(0, 32, unroll=8)
    def _(i):
        t = [jnp.maximum(s_ref[b, i + 32 * k], s_ref[b, 255 - i - 32 * k]) for k in range(4)]
        clean(t)
        for k in range(4):
            x_ref[h, i + 32 * k] = t[k]

    @pl.loop(0, 4)
    def _(k):
        x = clean([x_ref[h, k * 32 + i] for i in range(32)])
        for i in range(32):
            x_ref[h, k * 32 + i] = x[i]


def merge_pair(x_ref, b0, b1, level):
    bit = 1 << level
    lower = (lax.broadcasted_iota(jnp.int32, (SUBL, LANES), 0) & bit) == 0

    def joined(i, m):
        first = jnp.where(lower, x_ref[b0, i], x_ref[b1, i])
        second = jnp.where(lower, pltpu.roll(x_ref[b0, m], SUBL - bit, 0), pltpu.roll(x_ref[b1, m], bit, 0))
        return jnp.maximum(first, second)

    @pl.loop(0, 64, unroll=4)
    def _(i):
        m = 127 - i
        s, t = joined(i, m), joined(m, i)
        x_ref[b0, i] = s
        x_ref[b0, m] = t

    @pl.loop(0, 32, unroll=8)
    def _(i):
        t = clean([x_ref[b0, i + 32 * k] for k in range(4)])
        for k in range(4):
            x_ref[b0, i + 32 * k] = t[k]

    @pl.loop(0, 4)
    def _(k):
        x = clean([x_ref[b0, k * 32 + i] for i in range(32)])
        for i in range(32):
            x_ref[b0, k * 32 + i] = x[i]


def score_kernel(
    n_cap, idx_ref, sizes_ref, q_ref, own_ref, peer_ref, out_ref,
    s_ref, x_ref, z_ref, best_ref, back_ref, l_ref, send_sem, recv_sem, local_sem,
):
    p = pl.program_id(0)
    half = own_ref.shape[2]
    part_dev = pl.num_programs(0)
    all_rows = q_ref.shape[0]
    chip_slots = part_dev * n_cap
    n_dev = all_rows // chip_slots
    rep = lax.axis_index("rep")
    me = lax.axis_index("dom") * lax.axis_size("sub") + lax.axis_index("sub")
    barrier = pltpu.get_barrier_semaphore()

    @pl.when(p == 0)
    def _():
        @pl.loop(1, n_dev)
        def _(k):
            pl.semaphore_signal(barrier, inc=1, device_id=device_of((me + k) % n_dev), device_id_type=MESH)

    m = lax.broadcasted_iota(jnp.int32, (256, all_rows), 0)
    src = (m // 128) * 32 + m % 32
    want = src * chip_slots + p * n_cap + (m % 128) // 32
    pick = jnp.where(lax.broadcasted_iota(jnp.int32, (256, all_rows), 1) == want, 1.0, 0.0).astype(jnp.bfloat16)
    mine = jnp.dot(pick, q_ref[...], preferred_element_type=jnp.float32).astype(jnp.bfloat16)

    for which, ref in enumerate((own_ref, peer_ref)):
        sc = lax.dot_general(ref[0, 0], mine, (((1,), (1,)), ((), ())), preferred_element_type=jnp.float32)
        first = half * (rep if which == 0 else 1 - rep)
        ok = lax.broadcasted_iota(jnp.int32, (half, LANES), 0) + first < sizes_ref[p]
        for h in range(2):
            blk = jnp.where(ok, sc[:, h * LANES : (h + 1) * LANES], MASKED)
            s_ref[h, pl.ds(which * half // SUBL, half // SUBL)] = blk.reshape(half // SUBL, SUBL, LANES)

    for h in range(2):
        sort_block(s_ref, x_ref, h, p * 2 + h)

    @pl.when(p == part_dev - 1)
    def _():
        for b in range(0, 8, 2):
            merge_pair(x_ref, b, b + 1, 2)
        for b in range(0, 8, 4):
            merge_pair(x_ref, b, b + 2, 1)
        merge_pair(x_ref, 0, 4, 0)
        z_ref[...] = x_ref[0].reshape(RANKS * SUBL, LANES)
        for blk in range(8):
            u = 4 * (blk & 1) + (blk & 2) + (blk >> 2)
            got = z_ref[pl.ds(u, RANKS, stride=SUBL), :].T
            for r in range(n_cap):
                base = (blk & 1) * 32 * chip_slots + (blk >> 1) * n_cap + r
                best_ref[pl.ds(base, 32, stride=chip_slots), :] = got[r * 32 : (r + 1) * 32, :]

        def copy(k):
            t = (me + k) % n_dev
            return pltpu.make_async_remote_copy(
                src_ref=best_ref.at[pl.ds(pl.multiple_of(t * chip_slots, chip_slots), chip_slots)],
                dst_ref=back_ref.at[pl.ds(pl.multiple_of(me * chip_slots, chip_slots), chip_slots)],
                send_sem=send_sem.at[k],
                recv_sem=recv_sem.at[k],
                device_id=device_of(t),
                device_id_type=MESH,
            )

        pl.semaphore_wait(barrier, n_dev - 1)

        @pl.loop(1, n_dev)
        def _(k):
            copy(k).start()

        mine_rows = pl.ds(pl.multiple_of(me * chip_slots, chip_slots), chip_slots)
        keep = pltpu.make_async_copy(best_ref.at[mine_rows], back_ref.at[mine_rows], local_sem)
        keep.start()
        keep.wait()

        @pl.loop(1, n_dev)
        def _(k):
            copy(k).wait()

        final_merge(idx_ref, back_ref, l_ref, out_ref)


def final_merge(idx_ref, back_ref, l_ref, out_ref):
    n_probe, rows = idx_ref.shape
    for k in range(n_probe):

        @pl.loop(0, rows, unroll=8)
        def _(i):
            l_ref[pl.ds(k * rows + i, 1), :] = back_ref[pl.ds(idx_ref[k, i], 1), :]

    lists = l_ref[...]
    while lists.shape[0] > rows:
        h = lists.shape[0] // 2
        lane = lax.broadcasted_iota(jnp.int32, (h, RANKS), 1)
        a, b = lists[:h], lists[h:]
        lists = jnp.maximum(a, jnp.take_along_axis(b, RANKS - 1 - lane, axis=1))
        d = RANKS // 2
        while d:
            other = jnp.take_along_axis(lists, lane ^ d, axis=1)
            lists = jnp.where((lane & d) == 0, jnp.maximum(lists, other), jnp.minimum(lists, other))
            d //= 2
    out_ref[...] = lists[:, : out_ref.shape[1]]


def score(idx, sizes, rows, decoded, n_cap):
    _, part_dev, half, width = decoded.shape
    n_rows = rows.shape[0]
    n_probe, own_rows = idx.shape
    n_dev = n_rows // (part_dev * n_cap)
    return pl.pallas_call(
        functools.partial(score_kernel, n_cap),
        grid=(part_dev,),
        out_shape=jax.ShapeDtypeStruct((own_rows, TOPK), jnp.float32),
        in_specs=[
            pl.BlockSpec(memory_space=pltpu.SMEM),
            pl.BlockSpec(memory_space=pltpu.SMEM),
            pl.BlockSpec(memory_space=pltpu.VMEM),
            pl.BlockSpec((1, 1, half, width), lambda p: (0, p, 0, 0)),
            pl.BlockSpec((1, 1, half, width), lambda p: (1, p, 0, 0)),
        ],
        out_specs=pl.BlockSpec(memory_space=pltpu.VMEM),
        scratch_shapes=[
            pltpu.VMEM((2, 2 * half // SUBL, SUBL, LANES), jnp.float32),
            pltpu.VMEM((8, RANKS, SUBL, LANES), jnp.float32),
            pltpu.VMEM((RANKS * SUBL, LANES), jnp.float32),
            pltpu.VMEM((n_rows, RANKS), jnp.float32),
            pltpu.VMEM((n_rows, RANKS), jnp.float32),
            pltpu.VMEM((n_probe * own_rows, RANKS), jnp.float32),
            pltpu.SemaphoreType.DMA((n_dev,)),
            pltpu.SemaphoreType.DMA((n_dev,)),
            pltpu.SemaphoreType.DMA,
        ],
        compiler_params=pltpu.CompilerParams(collective_id=1, has_side_effects=True, vmem_limit_bytes=32 << 20),
        name="score",
    )(idx, sizes, rows, decoded, decoded)


def local(queries, codebook, probes, codes, part_sizes):
    n_dev = lax.axis_size("dom") * lax.axis_size("sub")
    own_rows, width = queries.shape
    n_probe = probes.shape[1]
    part_dev = codes.shape[0]
    n_parts = part_dev * n_dev
    n_cap = max(2, 2 * own_rows * n_probe // n_parts)
    arrived, idx, decoded = fetch(queries, probes.T, codebook.transpose(1, 2, 0), codes, n_dev, n_cap)
    return score(idx, part_sizes, arrived.reshape(n_parts * n_cap, width), decoded, n_cap)


def solution(mesh):
    in_specs = (
        P(("dom", "sub", "rep"), None),
        P(),
        P(("dom", "sub", "rep"), None),
        P(("dom", "sub"), None, "rep"),
        P(("dom", "sub")),
    )
    out_specs = P(("dom", "sub", "rep"), None)
    return jax.shard_map(local, mesh=mesh, in_specs=in_specs, out_specs=out_specs, check_vma=False)
```

```python
import functools

import jax
import jax.numpy as jnp
from jax import lax
from jax.experimental import pallas as pl
from jax.experimental.pallas import tpu as pltpu
from jax.sharding import PartitionSpec as P

TOPK = 100
MASKED = -1e30
RANKS = 128
LANES = 128
SUBL = 8


def batcher(n):
    pairs = []

    def merge(lo, cnt, r):
        step = r * 2
        if step < cnt:
            merge(lo, cnt, step)
            merge(lo + r, cnt, step)
            for i in range(lo + r, lo + cnt - r, step):
                pairs.append((i, i + r))
        else:
            pairs.append((lo, lo + r))

    def sort(lo, cnt):
        if cnt > 1:
            m = cnt // 2
            sort(lo, m)
            sort(lo + m, m)
            merge(lo, cnt, 1)

    sort(0, n)
    return pairs


SORT32 = batcher(32)


def exchange(x, pairs):
    for i, j in pairs:
        a, b = x[i], x[j]
        x[i] = jnp.maximum(a, b)
        x[j] = jnp.minimum(a, b)
    return x


def clean(x):
    d = len(x) // 2
    while d:
        exchange(x, [(i, i + d) for i in range(len(x)) if not i & d])
        d //= 2
    return x


MESH = pl.DeviceIdType.MESH


def device_of(t):
    n_sub = lax.axis_size("sub")
    return {"dom": t // n_sub, "sub": t % n_sub}


def route(n_cap, q_ref, probes_ref, send_ref, idx_ref):
    rows, width = q_ref.shape
    n_dev, chip_slots, _ = send_ref.shape
    slots = n_dev * chip_slots
    n = lax.broadcasted_iota(jnp.int32, (slots, rows), 0)
    part = n // n_cap
    rank_of = (n % n_cap).astype(jnp.float32)
    n_probe = probes_ref.shape[0]
    hits = [part == probes_ref[k : k + 1, :] for k in range(n_probe)]
    named = hits[0]
    for k in range(1, n_probe):
        named = named | hits[k]
    before = (
        lax.broadcasted_iota(jnp.int32, (rows, rows), 0) < lax.broadcasted_iota(jnp.int32, (rows, rows), 1)
    ).astype(jnp.float32).astype(jnp.bfloat16)
    rank = jnp.dot(named.astype(jnp.float32).astype(jnp.bfloat16), before, preferred_element_type=jnp.float32)
    chosen = named & (rank == rank_of)
    nf = jnp.where(chosen, n, 0)
    for k in range(n_probe):
        idx_ref[k : k + 1, :] = jnp.sum(jnp.where(hits[k], nf, 0), axis=0, keepdims=True)
    a = lax.broadcasted_iota(jnp.int32, (width, width), 0)
    b = lax.broadcasted_iota(jnp.int32, (width, width), 1)
    groups = width // 4
    j = (b >= groups).astype(jnp.int32) + (b >= 2 * groups).astype(jnp.int32) + (b >= 3 * groups).astype(jnp.int32)
    perm = jnp.where(a == (b - groups * j) * 4 + j, 1.0, 0.0).astype(jnp.bfloat16)
    moved = jnp.dot(q_ref[...], perm, preferred_element_type=jnp.float32).astype(jnp.bfloat16)
    pick = jnp.where(chosen, 1.0, 0.0).astype(jnp.bfloat16)
    picked = jnp.dot(pick, moved, preferred_element_type=jnp.float32)
    send_ref[...] = picked.astype(jnp.bfloat16).reshape(send_ref.shape)


def fill_table(book_ref, table_ref):
    n_cent, n_feat, groups = book_ref.shape
    for j in range(n_feat):
        plane = book_ref[:, j, :].astype(jnp.float32)
        wide = jnp.concatenate([plane, jnp.zeros((LANES - n_cent, groups), jnp.float32)], axis=0)
        table_ref[j] = wide.T


def decode(table_ref, codes_ref, p, t_ref, d_ref, slot):
    groups, half = codes_ref.shape[1:]

    @pl.loop(0, groups // 16)
    def _(g):
        rows = pl.ds(pl.multiple_of(g * 16, 16), 16)
        tab = [table_ref[j, rows, :] for j in range(4)]
        for t in range(half // LANES):
            cols = slice(t * LANES, (t + 1) * LANES)
            c = codes_ref[p, rows, cols]
            for j in range(4):
                val = jnp.take_along_axis(tab[j], c, axis=1)
                t_ref[pl.ds(pl.multiple_of(j * groups + g * 16, 16), 16), cols] = val.astype(jnp.bfloat16)

    @pl.loop(0, half // 256)
    def _(t):
        cols = pl.ds(pl.multiple_of(t * 256, 256), 256)
        d_ref[slot, cols, :] = t_ref[:, cols].T


def fetch_kernel(
    n_cap, q_in, probes_in, book_in, codes_ref, rows_ref, idx_ref, d_out,
    q_ref, probes_ref, book_ref, send_ref, own_ref, peer_ref, t_ref, d_ref, table_ref,
    small_sem, in_sem, out_sem, code_send, code_recv, row_send, row_recv, local_sem,
):
    n_dev = send_ref.shape[0]
    part_dev = codes_ref.shape[0]
    me = lax.axis_index("dom") * lax.axis_size("sub") + lax.axis_index("sub")
    other = {"rep": 1 - lax.axis_index("rep")}

    smalls = [
        pltpu.make_async_copy(src, dst, small_sem.at[i])
        for i, (src, dst) in enumerate(((q_in, q_ref), (probes_in, probes_ref), (book_in, book_ref)))
    ]
    for c in smalls:
        c.start()
    loads = [pltpu.make_async_copy(codes_ref.at[p], own_ref.at[p], in_sem.at[p]) for p in range(part_dev)]
    for c in loads:
        c.start()
    barrier = pltpu.get_barrier_semaphore()
    pl.semaphore_signal(barrier, inc=1, device_id=other, device_id_type=MESH)

    @pl.loop(1, n_dev)
    def _(k):
        pl.semaphore_signal(barrier, inc=1, device_id=device_of((me + k) % n_dev), device_id_type=MESH)

    smalls[0].wait()
    smalls[1].wait()
    route(n_cap, q_ref, probes_ref, send_ref, idx_ref)
    pl.semaphore_wait(barrier, n_dev)

    def row_copy(k):
        t = (me + k) % n_dev
        return pltpu.make_async_remote_copy(
            src_ref=send_ref.at[t],
            dst_ref=rows_ref.at[me],
            send_sem=row_send.at[k],
            recv_sem=row_recv.at[k],
            device_id=device_of(t),
            device_id_type=MESH,
        )

    @pl.loop(1, n_dev)
    def _(k):
        row_copy(k).start()

    swaps = [
        pltpu.make_async_remote_copy(
            src_ref=codes_ref.at[p],
            dst_ref=peer_ref.at[p],
            send_sem=code_send.at[p],
            recv_sem=code_recv.at[p],
            device_id=other,
            device_id_type=MESH,
        )
        for p in range(part_dev)
    ]
    for c in swaps:
        c.start()
    keep = pltpu.make_async_copy(send_ref.at[me], rows_ref.at[me], local_sem)
    keep.start()
    smalls[2].wait()
    fill_table(book_ref, table_ref)

    writes = []
    for which, ref in enumerate((own_ref, peer_ref)):
        for p in range(part_dev):
            n = which * part_dev + p
            if which == 0:
                loads[p].wait()
            else:
                swaps[p].wait()
            if n >= 2:
                writes[n - 2].wait()
            decode(table_ref, ref, p, t_ref, d_ref, n % 2)
            w = pltpu.make_async_copy(d_ref.at[n % 2], d_out.at[which, p], out_sem.at[n])
            w.start()
            writes.append(w)
    keep.wait()

    @pl.loop(1, n_dev)
    def _(k):
        row_copy(k).wait()

    writes[-2].wait()
    writes[-1].wait()


def fetch(queries, probes, book, codes, n_dev, n_cap):
    part_dev, groups, half = codes.shape
    width = queries.shape[1]
    vmem = pl.BlockSpec(memory_space=pltpu.VMEM)
    hbm = pl.BlockSpec(memory_space=pl.ANY)
    dma = pltpu.SemaphoreType.DMA
    return pl.pallas_call(
        functools.partial(fetch_kernel, n_cap),
        out_shape=(
            jax.ShapeDtypeStruct((n_dev, part_dev * n_cap, width), jnp.bfloat16),
            jax.ShapeDtypeStruct(probes.shape, jnp.int32),
            jax.ShapeDtypeStruct((2, part_dev, half, width), jnp.bfloat16),
        ),
        in_specs=[pl.BlockSpec(memory_space=pltpu.HBM)] * 4,
        out_specs=[hbm, vmem, hbm],
        scratch_shapes=[
            pltpu.VMEM(queries.shape, jnp.bfloat16),
            pltpu.VMEM(probes.shape, jnp.int32),
            pltpu.VMEM(book.shape, jnp.bfloat16),
            pltpu.VMEM((n_dev, part_dev * n_cap, width), jnp.bfloat16),
            pltpu.VMEM(codes.shape, jnp.int32),
            pltpu.VMEM(codes.shape, jnp.int32),
            pltpu.VMEM((width, half), jnp.bfloat16),
            pltpu.VMEM((2, half, width), jnp.bfloat16),
            pltpu.VMEM((book.shape[1], groups, LANES), jnp.float32),
            dma((3,)),
            dma((part_dev,)),
            dma((2 * part_dev,)),
            dma((part_dev,)),
            dma((part_dev,)),
            dma((n_dev,)),
            dma((n_dev,)),
            dma,
        ],
        compiler_params=pltpu.CompilerParams(collective_id=0, has_side_effects=True, vmem_limit_bytes=22 << 20),
        name="fetch",
    )(queries, probes, book, codes)


def sort_block(s_ref, x_ref, b, dst):
    @pl.loop(0, 8)
    def _(g):
        x = exchange([s_ref[b, g * 32 + i] for i in range(32)], SORT32)
        for i in range(32):
            s_ref[b, g * 32 + i] = x[i]

    @pl.loop(0, 4)
    def _(g):
        base = g * 64
        high = clean([jnp.maximum(s_ref[b, base + i], s_ref[b, base + 63 - i]) for i in range(32)])
        low = clean([jnp.minimum(s_ref[b, base + i], s_ref[b, base + 63 - i]) for i in range(32)])
        for i in range(32):
            s_ref[b, base + i] = high[i]
            s_ref[b, base + 32 + i] = low[i]

    @pl.loop(0, 2)
    def _(g):
        base = g * 128
        for i in range(32):
            u0, u1 = s_ref[b, base + i], s_ref[b, base + 32 + i]
            v0, v1 = s_ref[b, base + 127 - i], s_ref[b, base + 95 - i]
            h0, h1 = jnp.maximum(u0, v0), jnp.maximum(u1, v1)
            l0, l1 = jnp.minimum(u0, v0), jnp.minimum(u1, v1)
            x_ref[dst, i] = jnp.maximum(h0, h1)
            x_ref[dst, 32 + i] = jnp.minimum(h0, h1)
            x_ref[dst, 64 + i] = jnp.maximum(l0, l1)
            x_ref[dst, 96 + i] = jnp.minimum(l0, l1)

        @pl.loop(0, 4, unroll=2)
        def _(k):
            x = clean([x_ref[dst, k * 32 + i] for i in range(32)])
            for i in range(32):
                s_ref[b, base + k * 32 + i] = x[i]

    for i in range(32):
        t = clean([jnp.maximum(s_ref[b, i + 32 * k], s_ref[b, 255 - i - 32 * k]) for k in range(4)])
        for k in range(4):
            x_ref[dst, i + 32 * k] = t[k]

    @pl.loop(0, 4, unroll=2)
    def _(k):
        x = clean([x_ref[dst, k * 32 + i] for i in range(32)])
        for i in range(32):
            x_ref[dst, k * 32 + i] = x[i]


def merge_pair(x_ref, y_ref, b0, b1, dst, level):
    bit = 1 << level
    sublane = lax.broadcasted_iota(jnp.int32, (SUBL, LANES), 0)
    lower = (sublane & bit) == 0
    for i in range(16):
        first, second = {}, {}
        for j in [i + 32 * k for k in range(4)] + [31 - i + 32 * k for k in range(4)]:
            p, q = x_ref[b0, j], x_ref[b1, j]
            first[j] = jnp.where(lower, p, q)
            second[j] = jnp.take_along_axis(jnp.where(lower, q, p), sublane ^ bit, axis=0)
        for r in (i, 31 - i):
            t = clean([jnp.maximum(first[r + 32 * k], second[127 - r - 32 * k]) for k in range(4)])
            for k in range(4):
                y_ref[r + 32 * k] = t[k]

    @pl.loop(0, 4, unroll=2)
    def _(k):
        x = clean([y_ref[k * 32 + i] for i in range(32)])
        for i in range(32):
            x_ref[dst, k * 32 + i] = x[i]


def score_kernel(
    n_cap, idx_ref, sizes_ref, q_ref, own_ref, peer_ref, out_ref,
    s_ref, x_ref, y_ref, z_ref, best_ref, back_ref, l_ref, send_sem, recv_sem, local_sem,
):
    p = pl.program_id(0)
    half = own_ref.shape[2]
    part_dev = pl.num_programs(0)
    all_rows = q_ref.shape[0]
    chip_slots = part_dev * n_cap
    n_dev = all_rows // chip_slots
    rep = lax.axis_index("rep")
    me = lax.axis_index("dom") * lax.axis_size("sub") + lax.axis_index("sub")
    barrier = pltpu.get_barrier_semaphore()

    @pl.when(p == 0)
    def _():
        @pl.loop(1, n_dev)
        def _(k):
            pl.semaphore_signal(barrier, inc=1, device_id=device_of((me + k) % n_dev), device_id_type=MESH)

    m = lax.broadcasted_iota(jnp.int32, (256, all_rows), 0)
    src = (m // 128) * 32 + m % 32
    want = src * chip_slots + p * n_cap + (m % 128) // 32
    pick = jnp.where(lax.broadcasted_iota(jnp.int32, (256, all_rows), 1) == want, 1.0, 0.0).astype(jnp.bfloat16)
    mine = jnp.dot(pick, q_ref[...], preferred_element_type=jnp.float32).astype(jnp.bfloat16)

    for which, ref in enumerate((own_ref, peer_ref)):
        sc = lax.dot_general(ref[0, 0], mine, (((1,), (1,)), ((), ())), preferred_element_type=jnp.float32)
        first = half * (rep if which == 0 else 1 - rep)
        ok = lax.broadcasted_iota(jnp.int32, (half, LANES), 0) + first < sizes_ref[p]
        for h in range(2):
            blk = jnp.where(ok, sc[:, h * LANES : (h + 1) * LANES], MASKED)
            s_ref[h, pl.ds(which * half // SUBL, half // SUBL)] = blk.reshape(half // SUBL, SUBL, LANES)

    @pl.loop(0, 2)
    def _(h):
        sort_block(s_ref, x_ref, h, p * 2 + h)

    @pl.when(p == part_dev - 1)
    def _():
        @pl.loop(0, 4)
        def _(b):
            merge_pair(x_ref, y_ref, 2 * b, 2 * b + 1, b, 2)

        @pl.loop(0, 2)
        def _(b):
            merge_pair(x_ref, y_ref, 2 * b, 2 * b + 1, b, 1)

        merge_pair(x_ref, y_ref, 0, 1, 0, 0)
        z_ref[...] = x_ref[0].reshape(RANKS * SUBL, LANES)
        for blk in range(8):
            u = 4 * (blk & 1) + (blk & 2) + (blk >> 2)
            got = z_ref[pl.ds(u, RANKS, stride=SUBL), :].T
            for r in range(n_cap):
                base = (blk & 1) * 32 * chip_slots + (blk >> 1) * n_cap + r
                best_ref[pl.ds(base, 32, stride=chip_slots), :] = got[r * 32 : (r + 1) * 32, :]

        def copy(k):
            t = (me + k) % n_dev
            return pltpu.make_async_remote_copy(
                src_ref=best_ref.at[pl.ds(pl.multiple_of(t * chip_slots, chip_slots), chip_slots)],
                dst_ref=back_ref.at[pl.ds(pl.multiple_of(me * chip_slots, chip_slots), chip_slots)],
                send_sem=send_sem.at[k],
                recv_sem=recv_sem.at[k],
                device_id=device_of(t),
                device_id_type=MESH,
            )

        pl.semaphore_wait(barrier, n_dev - 1)

        @pl.loop(1, n_dev)
        def _(k):
            copy(k).start()

        mine_rows = pl.ds(pl.multiple_of(me * chip_slots, chip_slots), chip_slots)
        keep = pltpu.make_async_copy(best_ref.at[mine_rows], back_ref.at[mine_rows], local_sem)
        keep.start()
        keep.wait()

        @pl.loop(1, n_dev)
        def _(k):
            copy(k).wait()

        final_merge(idx_ref, back_ref, l_ref, out_ref)


def final_merge(idx_ref, back_ref, l_ref, out_ref):
    n_probe, rows = idx_ref.shape
    for k in range(n_probe):

        @pl.loop(0, rows, unroll=8)
        def _(i):
            l_ref[pl.ds(k * rows + i, 1), :] = back_ref[pl.ds(idx_ref[k, i], 1), :]

    lists = l_ref[...]
    while lists.shape[0] > rows:
        h = lists.shape[0] // 2
        lane = lax.broadcasted_iota(jnp.int32, (h, RANKS), 1)
        a, b = lists[:h], lists[h:]
        lists = jnp.maximum(a, jnp.take_along_axis(b, RANKS - 1 - lane, axis=1))
        d = RANKS // 2
        while d:
            other = jnp.take_along_axis(lists, lane ^ d, axis=1)
            lists = jnp.where((lane & d) == 0, jnp.maximum(lists, other), jnp.minimum(lists, other))
            d //= 2
    out_ref[...] = lists[:, : out_ref.shape[1]]


def score(idx, sizes, rows, decoded, n_cap):
    _, part_dev, half, width = decoded.shape
    n_rows = rows.shape[0]
    n_probe, own_rows = idx.shape
    n_dev = n_rows // (part_dev * n_cap)
    return pl.pallas_call(
        functools.partial(score_kernel, n_cap),
        grid=(part_dev,),
        out_shape=jax.ShapeDtypeStruct((own_rows, TOPK), jnp.float32),
        in_specs=[
            pl.BlockSpec(memory_space=pltpu.SMEM),
            pl.BlockSpec(memory_space=pltpu.SMEM),
            pl.BlockSpec(memory_space=pltpu.VMEM),
            pl.BlockSpec((1, 1, half, width), lambda p: (0, p, 0, 0)),
            pl.BlockSpec((1, 1, half, width), lambda p: (1, p, 0, 0)),
        ],
        out_specs=pl.BlockSpec(memory_space=pltpu.VMEM),
        scratch_shapes=[
            pltpu.VMEM((2, 2 * half // SUBL, SUBL, LANES), jnp.float32),
            pltpu.VMEM((8, RANKS, SUBL, LANES), jnp.float32),
            pltpu.VMEM((RANKS, SUBL, LANES), jnp.float32),
            pltpu.VMEM((RANKS * SUBL, LANES), jnp.float32),
            pltpu.VMEM((n_rows, RANKS), jnp.float32),
            pltpu.VMEM((n_rows, RANKS), jnp.float32),
            pltpu.VMEM((n_probe * own_rows, RANKS), jnp.float32),
            pltpu.SemaphoreType.DMA((n_dev,)),
            pltpu.SemaphoreType.DMA((n_dev,)),
            pltpu.SemaphoreType.DMA,
        ],
        compiler_params=pltpu.CompilerParams(collective_id=1, has_side_effects=True, vmem_limit_bytes=32 << 20),
        name="score",
    )(idx, sizes, rows, decoded, decoded)


def local(queries, codebook, probes, codes, part_sizes):
    n_dev = lax.axis_size("dom") * lax.axis_size("sub")
    own_rows, width = queries.shape
    n_probe = probes.shape[1]
    part_dev = codes.shape[0]
    n_parts = part_dev * n_dev
    n_cap = max(2, 2 * own_rows * n_probe // n_parts)
    args = (queries, probes.T, codebook.transpose(1, 2, 0), codes)
    args = [pltpu.with_memory_space_constraint(x, pltpu.HBM) for x in args]
    arrived, idx, decoded = fetch(*args, n_dev, n_cap)
    return score(idx, part_sizes, arrived.reshape(n_parts * n_cap, width), decoded, n_cap)


def solution(mesh):
    in_specs = (
        P(("dom", "sub", "rep"), None),
        P(),
        P(("dom", "sub", "rep"), None),
        P(("dom", "sub"), None, "rep"),
        P(("dom", "sub")),
    )
    out_specs = P(("dom", "sub", "rep"), None)
    return jax.shard_map(local, mesh=mesh, in_specs=in_specs, out_specs=out_specs, check_vma=False)
```

```python
import functools

import jax
import jax.numpy as jnp
from jax import lax
from jax.experimental import pallas as pl
from jax.experimental.pallas import tpu as pltpu
from jax.sharding import PartitionSpec as P

TOPK = 100
MASKED = -1e30
RANKS = 128
LANES = 128
SUBL = 8


def batcher(n):
    pairs = []

    def merge(lo, cnt, r):
        step = r * 2
        if step < cnt:
            merge(lo, cnt, step)
            merge(lo + r, cnt, step)
            for i in range(lo + r, lo + cnt - r, step):
                pairs.append((i, i + r))
        else:
            pairs.append((lo, lo + r))

    def sort(lo, cnt):
        if cnt > 1:
            m = cnt // 2
            sort(lo, m)
            sort(lo + m, m)
            merge(lo, cnt, 1)

    sort(0, n)
    return pairs


SORT32 = batcher(32)


def exchange(x, pairs):
    for i, j in pairs:
        a, b = x[i], x[j]
        x[i] = jnp.maximum(a, b)
        x[j] = jnp.minimum(a, b)
    return x


def clean(x):
    d = len(x) // 2
    while d:
        exchange(x, [(i, i + d) for i in range(len(x)) if not i & d])
        d //= 2
    return x


MESH = pl.DeviceIdType.MESH


def route(n_cap, q_ref, probes_ref, send_ref, idx_ref):
    rows, width = q_ref.shape
    chunks, n_dev, chip_slots, _ = send_ref.shape
    chunk_slots = n_dev * chip_slots
    slots = chunks * chunk_slots
    each = chip_slots // n_cap
    n = lax.broadcasted_iota(jnp.int32, (slots, rows), 0)
    chip = (n % chunk_slots) // chip_slots
    part = chip * (chunks * each) + (n // chunk_slots) * each + (n % chip_slots) // n_cap
    rank_of = (n % n_cap).astype(jnp.float32)
    n_probe = probes_ref.shape[0]
    hits = [part == probes_ref[k : k + 1, :] for k in range(n_probe)]
    named = hits[0]
    for k in range(1, n_probe):
        named = named | hits[k]
    before = (
        lax.broadcasted_iota(jnp.int32, (rows, rows), 0) < lax.broadcasted_iota(jnp.int32, (rows, rows), 1)
    ).astype(jnp.float32).astype(jnp.bfloat16)
    rank = jnp.dot(named.astype(jnp.float32).astype(jnp.bfloat16), before, preferred_element_type=jnp.float32)
    chosen = named & (rank == rank_of)
    nf = jnp.where(chosen, n, 0)
    for k in range(n_probe):
        idx_ref[k : k + 1, :] = jnp.sum(jnp.where(hits[k], nf, 0), axis=0, keepdims=True)
    a = lax.broadcasted_iota(jnp.int32, (width, width), 0)
    b = lax.broadcasted_iota(jnp.int32, (width, width), 1)
    groups = width // 4
    j = (b >= groups).astype(jnp.int32) + (b >= 2 * groups).astype(jnp.int32) + (b >= 3 * groups).astype(jnp.int32)
    perm = jnp.where(a == (b - groups * j) * 4 + j, 1.0, 0.0).astype(jnp.bfloat16)
    moved = jnp.dot(q_ref[...], perm, preferred_element_type=jnp.float32).astype(jnp.bfloat16)
    pick = jnp.where(chosen, 1.0, 0.0).astype(jnp.bfloat16)
    picked = jnp.dot(pick, moved, preferred_element_type=jnp.float32)
    send_ref[...] = picked.astype(jnp.bfloat16).reshape(send_ref.shape)


def fill_table(book_ref, table_ref):
    n_cent, n_feat, groups = book_ref.shape
    for j in range(n_feat):
        plane = book_ref[:, j, :].astype(jnp.float32)
        wide = jnp.concatenate([plane, jnp.zeros((LANES - n_cent, groups), jnp.float32)], axis=0)
        table_ref[j] = wide.T


def decode(table_ref, codes_ref, p, t_ref, d_ref):
    groups, half = codes_ref.shape[1:]

    @pl.loop(0, groups // 16)
    def _(g):
        rows = pl.ds(pl.multiple_of(g * 16, 16), 16)
        tab = [table_ref[j, rows, :] for j in range(4)]
        for t in range(half // LANES):
            cols = slice(t * LANES, (t + 1) * LANES)
            c = codes_ref[p, rows, cols]
            for j in range(4):
                val = jnp.take_along_axis(tab[j], c, axis=1)
                t_ref[pl.ds(pl.multiple_of(j * groups + g * 16, 16), 16), cols] = val.astype(jnp.bfloat16)

    @pl.loop(0, half // 256)
    def _(t):
        cols = pl.ds(pl.multiple_of(t * 256, 256), 256)
        d_ref[p, cols, :] = t_ref[:, cols].T


def sort_block(s_ref, x_ref, b, dst):
    @pl.loop(0, 8)
    def _(g):
        x = exchange([s_ref[b, g * 32 + i] for i in range(32)], SORT32)
        for i in range(32):
            s_ref[b, g * 32 + i] = x[i]

    @pl.loop(0, 4)
    def _(g):
        base = g * 64
        high = clean([jnp.maximum(s_ref[b, base + i], s_ref[b, base + 63 - i]) for i in range(32)])
        low = clean([jnp.minimum(s_ref[b, base + i], s_ref[b, base + 63 - i]) for i in range(32)])
        for i in range(32):
            s_ref[b, base + i] = high[i]
            s_ref[b, base + 32 + i] = low[i]

    @pl.loop(0, 2)
    def _(g):
        base = g * 128
        for i in range(32):
            u0, u1 = s_ref[b, base + i], s_ref[b, base + 32 + i]
            v0, v1 = s_ref[b, base + 127 - i], s_ref[b, base + 95 - i]
            h0, h1 = jnp.maximum(u0, v0), jnp.maximum(u1, v1)
            l0, l1 = jnp.minimum(u0, v0), jnp.minimum(u1, v1)
            x_ref[dst, i] = jnp.maximum(h0, h1)
            x_ref[dst, 32 + i] = jnp.minimum(h0, h1)
            x_ref[dst, 64 + i] = jnp.maximum(l0, l1)
            x_ref[dst, 96 + i] = jnp.minimum(l0, l1)

        @pl.loop(0, 4, unroll=2)
        def _(k):
            x = clean([x_ref[dst, k * 32 + i] for i in range(32)])
            for i in range(32):
                s_ref[b, base + k * 32 + i] = x[i]

    for i in range(32):
        t = clean([jnp.maximum(s_ref[b, i + 32 * k], s_ref[b, 255 - i - 32 * k]) for k in range(4)])
        for k in range(4):
            x_ref[dst, i + 32 * k] = t[k]

    @pl.loop(0, 4, unroll=2)
    def _(k):
        x = clean([x_ref[dst, k * 32 + i] for i in range(32)])
        for i in range(32):
            x_ref[dst, k * 32 + i] = x[i]


def merge_pair(x_ref, y_ref, b0, b1, dst, level):
    bit = 1 << level
    sublane = lax.broadcasted_iota(jnp.int32, (SUBL, LANES), 0)
    lower = (sublane & bit) == 0
    for i in range(16):
        first, second = {}, {}
        for j in [i + 32 * k for k in range(4)] + [31 - i + 32 * k for k in range(4)]:
            p, q = x_ref[b0, j], x_ref[b1, j]
            first[j] = jnp.where(lower, p, q)
            second[j] = jnp.take_along_axis(jnp.where(lower, q, p), sublane ^ bit, axis=0)
        for r in (i, 31 - i):
            t = clean([jnp.maximum(first[r + 32 * k], second[127 - r - 32 * k]) for k in range(4)])
            for k in range(4):
                y_ref[r + 32 * k] = t[k]

    @pl.loop(0, 4, unroll=2)
    def _(k):
        x = clean([y_ref[k * 32 + i] for i in range(32)])
        for i in range(32):
            x_ref[dst, k * 32 + i] = x[i]


def kernel(
    n_cap, sizes_ref, q_in, probes_in, book_in, codes_ref, out_ref,
    q_ref, probes_ref, book_ref, send_ref, rows_ref, own_ref, t_ref, d_own, d_peer, table_ref,
    s_ref, x_ref, y_ref, z_ref, best_ref, back_ref, l_ref, idx_vmem, idx_ref,
    small_sem, in_sem, code_send, code_recv, row_send, row_recv, best_send, best_recv, row_keep, best_keep,
):
    chunks, n_dev, chip_slots, width = send_ref.shape
    part_dev, _, half = codes_ref.shape
    each = part_dev // chunks
    rep = lax.axis_index("rep")
    n_sub, n_dom = lax.axis_size("sub"), lax.axis_size("dom")
    my_dom, my_sub = lax.axis_index("dom"), lax.axis_index("sub")
    me = my_dom * n_sub + my_sub
    other = {"rep": 1 - rep}

    smalls = [
        pltpu.make_async_copy(src, dst, small_sem.at[i])
        for i, (src, dst) in enumerate(((q_in, q_ref), (probes_in, probes_ref), (book_in, book_ref)))
    ]
    for c in smalls:
        c.start()
    loads = [pltpu.make_async_copy(codes_ref.at[p], own_ref.at[p], in_sem.at[p]) for p in range(part_dev)]
    for c in loads:
        c.start()
    barrier = pltpu.get_barrier_semaphore()
    pl.semaphore_signal(barrier, inc=1, device_id=other, device_id_type=MESH)

    def partners(visit):
        for ks in range(1, n_sub):
            visit(my_dom, lax.rem(my_sub + ks, n_sub))

        @pl.loop(1, n_dom)
        def _(kd):
            for ks in range(n_sub):
                visit(lax.rem(my_dom + kd, n_dom), lax.rem(my_sub + ks, n_sub))

    @partners
    def _(td, ts):
        pl.semaphore_signal(barrier, inc=1, device_id={"dom": td, "sub": ts}, device_id_type=MESH)

    for c in smalls:
        c.wait()
    route(n_cap, q_ref, probes_ref, send_ref, idx_vmem)
    fill_table(book_ref, table_ref)
    pl.semaphore_wait(barrier, n_dev)

    def exchange_all(src, dst, send_sem, recv_sem, keep_sem):
        @partners
        def _(td, ts):
            pltpu.make_async_remote_copy(
                src_ref=src.at[td * n_sub + ts],
                dst_ref=dst.at[me],
                send_sem=send_sem,
                recv_sem=recv_sem,
                device_id={"dom": td, "sub": ts},
                device_id_type=MESH,
            ).start()

        pltpu.make_async_copy(src.at[me], dst.at[me], keep_sem).start()

    def finish_recv(src, dst, recv_sem, keep_sem):
        most = pl.ds(0, n_dev - 1)
        pltpu.make_async_copy(src.at[most], dst.at[most], recv_sem).wait()
        pltpu.make_async_copy(src.at[me], dst.at[me], keep_sem).wait()

    def finish_send(src, dst, send_sem):
        most = pl.ds(0, n_dev - 1)
        pltpu.make_async_copy(src.at[most], dst.at[most], send_sem).wait()

    swaps = [
        pltpu.make_async_remote_copy(
            src_ref=d_own.at[p],
            dst_ref=d_peer.at[p],
            send_sem=code_send.at[p],
            recv_sem=code_recv.at[p],
            device_id=other,
            device_id_type=MESH,
        )
        for p in range(part_dev)
    ]
    for c in range(chunks):
        exchange_all(send_ref.at[c], rows_ref.at[c], row_send.at[c], row_recv.at[c], row_keep.at[c])
        for p in range(c * each, (c + 1) * each):
            loads[p].wait()
            decode(table_ref, own_ref, p, t_ref, d_own)
            swaps[p].start()
    for_idx = pltpu.make_async_copy(idx_vmem, idx_ref, small_sem.at[0])
    for_idx.start()

    for c in range(chunks):
        finish_recv(send_ref.at[c], rows_ref.at[c], row_recv.at[c], row_keep.at[c])
        rows = rows_ref[c].reshape(n_dev * chip_slots, width)
        for e in range(each):
            p = c * each + e
            m = lax.broadcasted_iota(jnp.int32, (256, rows.shape[0]), 0)
            want = ((m // 128) * 32 + m % 32) * chip_slots + e * n_cap + (m % 128) // 32
            pick = jnp.where(lax.broadcasted_iota(jnp.int32, m.shape, 1) == want, 1.0, 0.0).astype(jnp.bfloat16)
            mine = jnp.dot(pick, rows, preferred_element_type=jnp.float32).astype(jnp.bfloat16)
            for which, ref in enumerate((d_own, d_peer)):
                if which == 1:
                    swaps[p].wait_recv()
                sc = lax.dot_general(ref[p], mine, (((1,), (1,)), ((), ())), preferred_element_type=jnp.float32)
                first = half * (rep if which == 0 else 1 - rep)
                ok = lax.broadcasted_iota(jnp.int32, (half, LANES), 0) + first < sizes_ref[p]
                for h in range(2):
                    blk = jnp.where(ok, sc[:, h * LANES : (h + 1) * LANES], MASKED)
                    s_ref[h, pl.ds(which * half // SUBL, half // SUBL)] = blk.reshape(half // SUBL, SUBL, LANES)

            @pl.loop(0, 2)
            def _(h):
                sort_block(s_ref, x_ref, h, e * 2 + h)

        @pl.loop(0, 2)
        def _(b):
            merge_pair(x_ref, y_ref, 2 * b, 2 * b + 1, b, 2)

        merge_pair(x_ref, y_ref, 0, 1, 0, 1)
        merge_pair(x_ref, y_ref, 0, 0, 0, 0)
        z_ref[...] = x_ref[0].reshape(RANKS * SUBL, LANES)
        for blk in range(4):
            u = 4 * (blk & 1) + (blk & 2)
            got = z_ref[pl.ds(u, RANKS, stride=SUBL), :].T
            for r in range(n_cap):
                slot = (blk >> 1) * n_cap + r
                best_ref[c, (blk & 1) * 32 : (blk & 1) * 32 + 32, slot, :] = got[r * 32 : (r + 1) * 32, :]
        exchange_all(best_ref.at[c], back_ref.at[c], best_send.at[c], best_recv.at[c], best_keep.at[c])

    for_idx.wait()
    for c in range(chunks):
        finish_recv(best_ref.at[c], back_ref.at[c], best_recv.at[c], best_keep.at[c])
    final_merge(idx_ref, back_ref, l_ref, out_ref)
    for c in range(chunks):
        finish_send(send_ref.at[c], rows_ref.at[c], row_send.at[c])
        finish_send(best_ref.at[c], back_ref.at[c], best_send.at[c])
    for c in swaps:
        c.wait_send()


def final_merge(idx_ref, back_ref, l_ref, out_ref):
    n_probe, rows = idx_ref.shape
    flat = back_ref.reshape(l_ref.shape[0] * 2, RANKS)
    for k in range(n_probe):

        @pl.loop(0, rows, unroll=8)
        def _(i):
            n = idx_ref[k, i]
            l_ref[pl.ds(k * rows + i, 1), :] = flat[pl.ds(n, 1), :]

    lists = l_ref[...]
    while lists.shape[0] > rows:
        h = lists.shape[0] // 2
        lane = lax.broadcasted_iota(jnp.int32, (h, RANKS), 1)
        a, b = lists[:h], lists[h:]
        lists = jnp.maximum(a, jnp.take_along_axis(b, RANKS - 1 - lane, axis=1))
        d = RANKS // 2
        while d:
            other = jnp.take_along_axis(lists, lane ^ d, axis=1)
            lists = jnp.where((lane & d) == 0, jnp.maximum(lists, other), jnp.minimum(lists, other))
            d //= 2
    out_ref[...] = lists[:, : out_ref.shape[1]]


def local(queries, codebook, probes, codes, part_sizes):
    n_dev = lax.axis_size("dom") * lax.axis_size("sub")
    own_rows, width = queries.shape
    n_probe = probes.shape[1]
    part_dev, groups, half = codes.shape
    n_cap = max(2, 2 * own_rows * n_probe // (part_dev * n_dev))
    chunks = 2
    chip_slots = part_dev * n_cap // chunks
    book = codebook.transpose(1, 2, 0)
    args = [pltpu.with_memory_space_constraint(x, pltpu.HBM) for x in (queries, probes.T, book, codes)]
    hbm = pl.BlockSpec(memory_space=pltpu.HBM)
    vmem, dma = pltpu.VMEM, pltpu.SemaphoreType.DMA
    lists = vmem((chunks, n_dev, chip_slots, RANKS), jnp.float32)
    rows = vmem((chunks, n_dev, chip_slots, width), jnp.bfloat16)
    decoded = vmem((part_dev, half, width), jnp.bfloat16)
    return pl.pallas_call(
        functools.partial(kernel, n_cap),
        out_shape=jax.ShapeDtypeStruct((own_rows, TOPK), jnp.float32),
        in_specs=[pl.BlockSpec(memory_space=pltpu.SMEM), hbm, hbm, hbm, hbm],
        out_specs=pl.BlockSpec(memory_space=pltpu.VMEM),
        scratch_shapes=[
            vmem(queries.shape, jnp.bfloat16),
            vmem((n_probe, own_rows), jnp.int32),
            vmem(book.shape, jnp.bfloat16),
            rows,
            rows,
            vmem(codes.shape, jnp.int32),
            vmem((width, half), jnp.bfloat16),
            decoded,
            decoded,
            vmem((book.shape[1], groups, LANES), jnp.float32),
            vmem((2, 2 * half // SUBL, SUBL, LANES), jnp.float32),
            vmem((4, RANKS, SUBL, LANES), jnp.float32),
            vmem((RANKS, SUBL, LANES), jnp.float32),
            vmem((RANKS * SUBL, LANES), jnp.float32),
            lists,
            lists,
            vmem((n_probe * own_rows, RANKS), jnp.float32),
            vmem((n_probe, own_rows), jnp.int32),
            pltpu.SMEM((n_probe, own_rows), jnp.int32),
            dma((3,)),
            dma((part_dev,)),
            dma((part_dev,)),
            dma((part_dev,)),
            dma((chunks,)),
            dma((chunks,)),
            dma((chunks,)),
            dma((chunks,)),
            dma((chunks,)),
            dma((chunks,)),
        ],
        compiler_params=pltpu.CompilerParams(collective_id=0, has_side_effects=True, vmem_limit_bytes=56 << 20),
        name="search",
    )(part_sizes, *args)


def solution(mesh):
    in_specs = (
        P(("dom", "sub", "rep"), None),
        P(),
        P(("dom", "sub", "rep"), None),
        P(("dom", "sub"), None, "rep"),
        P(("dom", "sub")),
    )
    out_specs = P(("dom", "sub", "rep"), None)
    return jax.shard_map(local, mesh=mesh, in_specs=in_specs, out_specs=out_specs, check_vma=False)
```

```python
import functools

import jax
import jax.numpy as jnp
from jax import lax
from jax.experimental import pallas as pl
from jax.experimental.pallas import tpu as pltpu
from jax.sharding import PartitionSpec as P

TOPK = 100
MASKED = -1e30
RANKS = 128
LANES = 128
SUBL = 8


def batcher(n):
    pairs = []

    def merge(lo, cnt, r):
        step = r * 2
        if step < cnt:
            merge(lo, cnt, step)
            merge(lo + r, cnt, step)
            for i in range(lo + r, lo + cnt - r, step):
                pairs.append((i, i + r))
        else:
            pairs.append((lo, lo + r))

    def sort(lo, cnt):
        if cnt > 1:
            m = cnt // 2
            sort(lo, m)
            sort(lo + m, m)
            merge(lo, cnt, 1)

    sort(0, n)
    return pairs


SORT32 = batcher(32)


def exchange(x, pairs):
    for i, j in pairs:
        a, b = x[i], x[j]
        x[i] = jnp.maximum(a, b)
        x[j] = jnp.minimum(a, b)
    return x


def clean(x):
    d = len(x) // 2
    while d:
        exchange(x, [(i, i + d) for i in range(len(x)) if not i & d])
        d //= 2
    return x


MESH = pl.DeviceIdType.MESH


def route(n_cap, q_ref, probes_ref, send_ref, idx_ref):
    rows, width = q_ref.shape
    chunks, n_dev, chip_slots, _ = send_ref.shape
    chunk_slots = n_dev * chip_slots
    slots = chunks * chunk_slots
    each = chip_slots // n_cap
    n = lax.broadcasted_iota(jnp.int32, (slots, rows), 0)
    chip = (n % chunk_slots) // chip_slots
    part = chip * (chunks * each) + (n // chunk_slots) * each + (n % chip_slots) // n_cap
    rank_of = (n % n_cap).astype(jnp.float32)
    n_probe = probes_ref.shape[0]
    hits = [part == probes_ref[k : k + 1, :] for k in range(n_probe)]
    named = hits[0]
    for k in range(1, n_probe):
        named = named | hits[k]
    before = (
        lax.broadcasted_iota(jnp.int32, (rows, rows), 0) < lax.broadcasted_iota(jnp.int32, (rows, rows), 1)
    ).astype(jnp.float32).astype(jnp.bfloat16)
    rank = jnp.dot(named.astype(jnp.float32).astype(jnp.bfloat16), before, preferred_element_type=jnp.float32)
    chosen = named & (rank == rank_of)
    nf = jnp.where(chosen, n, 0)
    for k in range(n_probe):
        idx_ref[k : k + 1, :] = jnp.sum(jnp.where(hits[k], nf, 0), axis=0, keepdims=True)
    a = lax.broadcasted_iota(jnp.int32, (width, width), 0)
    b = lax.broadcasted_iota(jnp.int32, (width, width), 1)
    groups = width // 4
    j = (b >= groups).astype(jnp.int32) + (b >= 2 * groups).astype(jnp.int32) + (b >= 3 * groups).astype(jnp.int32)
    perm = jnp.where(a == (b - groups * j) * 4 + j, 1.0, 0.0).astype(jnp.bfloat16)
    moved = jnp.dot(q_ref[...], perm, preferred_element_type=jnp.float32).astype(jnp.bfloat16)
    pick = jnp.where(chosen, 1.0, 0.0).astype(jnp.bfloat16)
    picked = jnp.dot(pick, moved, preferred_element_type=jnp.float32)
    send_ref[...] = picked.astype(jnp.bfloat16).reshape(send_ref.shape)


def fill_table(book_ref, table_ref):
    n_cent, n_feat, groups = book_ref.shape
    for j in range(n_feat):
        plane = book_ref[:, j, :].astype(jnp.float32)
        wide = jnp.concatenate([plane, jnp.zeros((LANES - n_cent, groups), jnp.float32)], axis=0)
        table_ref[j] = wide.T


def decode(table_ref, codes_ref, p, t_ref, d_ref):
    groups, half = codes_ref.shape[1:]

    @pl.loop(0, groups // 16)
    def _(g):
        rows = pl.ds(pl.multiple_of(g * 16, 16), 16)
        tab = [table_ref[j, rows, :] for j in range(4)]
        for t in range(half // LANES):
            cols = slice(t * LANES, (t + 1) * LANES)
            c = codes_ref[p, rows, cols]
            for j in range(4):
                val = jnp.take_along_axis(tab[j], c, axis=1)
                t_ref[pl.ds(pl.multiple_of(j * groups + g * 16, 16), 16), cols] = val.astype(jnp.bfloat16)

    @pl.loop(0, half // 256)
    def _(t):
        cols = pl.ds(pl.multiple_of(t * 256, 256), 256)
        d_ref[p, cols, :] = t_ref[:, cols].T


def sort_block(s_ref, x_ref, b, dst):
    @pl.loop(0, 8)
    def _(g):
        x = exchange([s_ref[b, g * 32 + i] for i in range(32)], SORT32)
        for i in range(32):
            s_ref[b, g * 32 + i] = x[i]

    @pl.loop(0, 4)
    def _(g):
        base = g * 64
        high = clean([jnp.maximum(s_ref[b, base + i], s_ref[b, base + 63 - i]) for i in range(32)])
        low = clean([jnp.minimum(s_ref[b, base + i], s_ref[b, base + 63 - i]) for i in range(32)])
        for i in range(32):
            s_ref[b, base + i] = high[i]
            s_ref[b, base + 32 + i] = low[i]

    @pl.loop(0, 2)
    def _(g):
        base = g * 128
        for i in range(32):
            u0, u1 = s_ref[b, base + i], s_ref[b, base + 32 + i]
            v0, v1 = s_ref[b, base + 127 - i], s_ref[b, base + 95 - i]
            h0, h1 = jnp.maximum(u0, v0), jnp.maximum(u1, v1)
            l0, l1 = jnp.minimum(u0, v0), jnp.minimum(u1, v1)
            x_ref[dst, i] = jnp.maximum(h0, h1)
            x_ref[dst, 32 + i] = jnp.minimum(h0, h1)
            x_ref[dst, 64 + i] = jnp.maximum(l0, l1)
            x_ref[dst, 96 + i] = jnp.minimum(l0, l1)

        @pl.loop(0, 4, unroll=2)
        def _(k):
            x = clean([x_ref[dst, k * 32 + i] for i in range(32)])
            for i in range(32):
                s_ref[b, base + k * 32 + i] = x[i]

    for i in range(32):
        t = clean([jnp.maximum(s_ref[b, i + 32 * k], s_ref[b, 255 - i - 32 * k]) for k in range(4)])
        for k in range(4):
            x_ref[dst, i + 32 * k] = t[k]

    @pl.loop(0, 4, unroll=2)
    def _(k):
        x = clean([x_ref[dst, k * 32 + i] for i in range(32)])
        for i in range(32):
            x_ref[dst, k * 32 + i] = x[i]


def merge_pair(x_ref, y_ref, b0, b1, dst, level):
    bit = 1 << level
    sublane = lax.broadcasted_iota(jnp.int32, (SUBL, LANES), 0)
    lower = (sublane & bit) == 0
    for i in range(16):
        first, second = {}, {}
        for j in [i + 32 * k for k in range(4)] + [31 - i + 32 * k for k in range(4)]:
            p, q = x_ref[b0, j], x_ref[b1, j]
            first[j] = jnp.where(lower, p, q)
            second[j] = jnp.take_along_axis(jnp.where(lower, q, p), sublane ^ bit, axis=0)
        for r in (i, 31 - i):
            t = clean([jnp.maximum(first[r + 32 * k], second[127 - r - 32 * k]) for k in range(4)])
            for k in range(4):
                y_ref[r + 32 * k] = t[k]

    @pl.loop(0, 4, unroll=2)
    def _(k):
        x = clean([y_ref[k * 32 + i] for i in range(32)])
        for i in range(32):
            x_ref[dst, k * 32 + i] = x[i]


def kernel(
    n_cap, sizes_in, q_in, probes_in, book_in, codes_ref, out_ref,
    sizes_ref, q_ref, probes_ref, book_ref, send_ref, rows_ref, own_ref, t_ref, d_own, d_peer, table_ref,
    s_ref, x_ref, y_ref, z_ref, best_ref, back_ref, l_ref, idx_vmem, idx_ref,
    small_sem, in_sem, code_send, code_recv, row_send, row_recv, best_send, best_recv, row_keep, best_keep,
):
    chunks, n_dev, chip_slots, width = send_ref.shape
    part_dev, _, half = codes_ref.shape
    each = part_dev // chunks
    rep = lax.axis_index("rep")
    n_sub, n_dom = lax.axis_size("sub"), lax.axis_size("dom")
    my_dom, my_sub = lax.axis_index("dom"), lax.axis_index("sub")
    me = my_dom * n_sub + my_sub
    other = {"rep": 1 - rep}

    smalls = [
        pltpu.make_async_copy(src, dst, small_sem.at[i])
        for i, (src, dst) in enumerate(
            ((q_in, q_ref), (probes_in, probes_ref), (book_in, book_ref), (sizes_in, sizes_ref))
        )
    ]
    for c in smalls:
        c.start()
    loads = [pltpu.make_async_copy(codes_ref.at[p], own_ref.at[p], in_sem.at[p]) for p in range(part_dev)]
    for c in loads:
        c.start()
    barrier = pltpu.get_barrier_semaphore()
    pl.semaphore_signal(barrier, inc=1, device_id=other, device_id_type=MESH)

    def partners(visit):
        for ks in range(1, n_sub):
            visit(my_dom, lax.rem(my_sub + ks, n_sub))

        @pl.loop(1, n_dom)
        def _(kd):
            for ks in range(n_sub):
                visit(lax.rem(my_dom + kd, n_dom), lax.rem(my_sub + ks, n_sub))

    @partners
    def _(td, ts):
        pl.semaphore_signal(barrier, inc=1, device_id={"dom": td, "sub": ts}, device_id_type=MESH)

    for c in smalls:
        c.wait()
    route(n_cap, q_ref, probes_ref, send_ref, idx_vmem)
    fill_table(book_ref, table_ref)
    pl.semaphore_wait(barrier, n_dev)

    def exchange_all(src, dst, send_sem, recv_sem, keep_sem):
        @partners
        def _(td, ts):
            pltpu.make_async_remote_copy(
                src_ref=src.at[td * n_sub + ts],
                dst_ref=dst.at[me],
                send_sem=send_sem,
                recv_sem=recv_sem,
                device_id={"dom": td, "sub": ts},
                device_id_type=MESH,
            ).start()

        pltpu.make_async_copy(src.at[me], dst.at[me], keep_sem).start()

    def finish_recv(src, dst, recv_sem, keep_sem):
        most = pl.ds(0, n_dev - 1)
        pltpu.make_async_copy(src.at[most], dst.at[most], recv_sem).wait()
        pltpu.make_async_copy(src.at[me], dst.at[me], keep_sem).wait()

    def finish_send(src, dst, send_sem):
        most = pl.ds(0, n_dev - 1)
        pltpu.make_async_copy(src.at[most], dst.at[most], send_sem).wait()

    swaps = [
        pltpu.make_async_remote_copy(
            src_ref=d_own.at[p],
            dst_ref=d_peer.at[p],
            send_sem=code_send.at[p],
            recv_sem=code_recv.at[p],
            device_id=other,
            device_id_type=MESH,
        )
        for p in range(part_dev)
    ]
    def send_rows(c):
        exchange_all(send_ref.at[c], rows_ref.at[c], row_send.at[c], row_recv.at[c], row_keep.at[c])

    send_rows(0)
    for p in range(part_dev):
        loads[p].wait()
        decode(table_ref, own_ref, p, t_ref, d_own)
        if p < each:
            swaps[p].start()
    send_rows(1)
    for_idx = pltpu.make_async_copy(idx_vmem, idx_ref, small_sem.at[0])
    for_idx.start()

    for c in range(chunks):
        finish_recv(send_ref.at[c], rows_ref.at[c], row_recv.at[c], row_keep.at[c])
        if c == 0:
            for p in range(each, part_dev):
                swaps[p].start()
        rows = rows_ref[c].reshape(n_dev * chip_slots, width)
        for e in range(each):
            p = c * each + e
            m = lax.broadcasted_iota(jnp.int32, (256, rows.shape[0]), 0)
            want = ((m // 128) * 32 + m % 32) * chip_slots + e * n_cap + (m % 128) // 32
            pick = jnp.where(lax.broadcasted_iota(jnp.int32, m.shape, 1) == want, 1.0, 0.0).astype(jnp.bfloat16)
            mine = jnp.dot(pick, rows, preferred_element_type=jnp.float32).astype(jnp.bfloat16)
            for which, ref in enumerate((d_own, d_peer)):
                if which == 1:
                    swaps[p].wait_recv()
                sc = lax.dot_general(ref[p], mine, (((1,), (1,)), ((), ())), preferred_element_type=jnp.float32)
                first = half * (rep if which == 0 else 1 - rep)
                ok = lax.broadcasted_iota(jnp.int32, (half, LANES), 0) + first < sizes_ref[p]
                for h in range(2):
                    blk = jnp.where(ok, sc[:, h * LANES : (h + 1) * LANES], MASKED)
                    s_ref[h, pl.ds(which * half // SUBL, half // SUBL)] = blk.reshape(half // SUBL, SUBL, LANES)

            @pl.loop(0, 2)
            def _(h):
                sort_block(s_ref, x_ref, h, e * 2 + h)

        @pl.loop(0, 2)
        def _(b):
            merge_pair(x_ref, y_ref, 2 * b, 2 * b + 1, b, 2)

        merge_pair(x_ref, y_ref, 0, 1, 0, 1)
        merge_pair(x_ref, y_ref, 0, 0, 0, 0)
        z_ref[...] = x_ref[0].reshape(RANKS * SUBL, LANES)
        for blk in range(4):
            u = 4 * (blk & 1) + (blk & 2)
            got = z_ref[pl.ds(u, RANKS, stride=SUBL), :].T
            for r in range(n_cap):
                slot = (blk >> 1) * n_cap + r
                best_ref[c, (blk & 1) * 32 : (blk & 1) * 32 + 32, slot, :] = got[r * 32 : (r + 1) * 32, :]
        exchange_all(best_ref.at[c], back_ref.at[c], best_send.at[c], best_recv.at[c], best_keep.at[c])

    for_idx.wait()
    for c in range(chunks):
        finish_recv(best_ref.at[c], back_ref.at[c], best_recv.at[c], best_keep.at[c])
    final_merge(idx_ref, back_ref, l_ref, out_ref)
    for c in range(chunks):
        finish_send(send_ref.at[c], rows_ref.at[c], row_send.at[c])
        finish_send(best_ref.at[c], back_ref.at[c], best_send.at[c])
    for c in swaps:
        c.wait_send()


def final_merge(idx_ref, back_ref, l_ref, out_ref):
    n_probe, rows = idx_ref.shape
    flat = back_ref.reshape(l_ref.shape[0] * 2, RANKS)
    for k in range(n_probe):

        @pl.loop(0, rows, unroll=8)
        def _(i):
            n = idx_ref[k, i]
            l_ref[pl.ds(k * rows + i, 1), :] = flat[pl.ds(n, 1), :]

    lists = l_ref[...]
    while lists.shape[0] > rows:
        h = lists.shape[0] // 2
        lane = lax.broadcasted_iota(jnp.int32, (h, RANKS), 1)
        a, b = lists[:h], lists[h:]
        lists = jnp.maximum(a, jnp.take_along_axis(b, RANKS - 1 - lane, axis=1))
        d = RANKS // 2
        while d:
            other = jnp.take_along_axis(lists, lane ^ d, axis=1)
            lists = jnp.where((lane & d) == 0, jnp.maximum(lists, other), jnp.minimum(lists, other))
            d //= 2
    out_ref[...] = lists[:, : out_ref.shape[1]]


def local(queries, codebook, probes, codes, part_sizes):
    n_dev = lax.axis_size("dom") * lax.axis_size("sub")
    own_rows, width = queries.shape
    n_probe = probes.shape[1]
    part_dev, groups, half = codes.shape
    n_cap = max(2, 2 * own_rows * n_probe // (part_dev * n_dev))
    chunks = 2
    chip_slots = part_dev * n_cap // chunks
    book = codebook.transpose(1, 2, 0)
    args = [pltpu.with_memory_space_constraint(x, pltpu.HBM) for x in (part_sizes, queries, probes.T, book, codes)]
    hbm = pl.BlockSpec(memory_space=pltpu.HBM)
    vmem, dma = pltpu.VMEM, pltpu.SemaphoreType.DMA
    lists = vmem((chunks, n_dev, chip_slots, RANKS), jnp.float32)
    rows = vmem((chunks, n_dev, chip_slots, width), jnp.bfloat16)
    decoded = vmem((part_dev, half, width), jnp.bfloat16)
    return pl.pallas_call(
        functools.partial(kernel, n_cap),
        out_shape=jax.ShapeDtypeStruct((own_rows, TOPK), jnp.float32),
        in_specs=[hbm] * 5,
        out_specs=pl.BlockSpec(memory_space=pltpu.VMEM),
        scratch_shapes=[
            pltpu.SMEM(part_sizes.shape, jnp.int32),
            vmem(queries.shape, jnp.bfloat16),
            vmem((n_probe, own_rows), jnp.int32),
            vmem(book.shape, jnp.bfloat16),
            rows,
            rows,
            vmem(codes.shape, jnp.int32),
            vmem((width, half), jnp.bfloat16),
            decoded,
            decoded,
            vmem((book.shape[1], groups, LANES), jnp.float32),
            vmem((2, 2 * half // SUBL, SUBL, LANES), jnp.float32),
            vmem((4, RANKS, SUBL, LANES), jnp.float32),
            vmem((RANKS, SUBL, LANES), jnp.float32),
            vmem((RANKS * SUBL, LANES), jnp.float32),
            lists,
            lists,
            vmem((n_probe * own_rows, RANKS), jnp.float32),
            vmem((n_probe, own_rows), jnp.int32),
            pltpu.SMEM((n_probe, own_rows), jnp.int32),
            dma((4,)),
            dma((part_dev,)),
            dma((part_dev,)),
            dma((part_dev,)),
            dma((chunks,)),
            dma((chunks,)),
            dma((chunks,)),
            dma((chunks,)),
            dma((chunks,)),
            dma((chunks,)),
        ],
        compiler_params=pltpu.CompilerParams(collective_id=0, has_side_effects=True, vmem_limit_bytes=40 << 20),
        name="search",
    )(*args)


def solution(mesh):
    in_specs = (
        P(("dom", "sub", "rep"), None),
        P(),
        P(("dom", "sub", "rep"), None),
        P(("dom", "sub"), None, "rep"),
        P(("dom", "sub")),
    )
    out_specs = P(("dom", "sub", "rep"), None)
    return jax.shard_map(local, mesh=mesh, in_specs=in_specs, out_specs=out_specs, check_vma=False)
```

```python
import functools

import jax
import jax.numpy as jnp
from jax import lax
from jax.experimental import pallas as pl
from jax.experimental.pallas import tpu as pltpu
from jax.sharding import PartitionSpec as P

TOPK = 100
MASKED = -1e30
RANKS = 128
LANES = 128
SUBL = 8


def batcher(n):
    pairs = []

    def merge(lo, cnt, r):
        step = r * 2
        if step < cnt:
            merge(lo, cnt, step)
            merge(lo + r, cnt, step)
            for i in range(lo + r, lo + cnt - r, step):
                pairs.append((i, i + r))
        else:
            pairs.append((lo, lo + r))

    def sort(lo, cnt):
        if cnt > 1:
            m = cnt // 2
            sort(lo, m)
            sort(lo + m, m)
            merge(lo, cnt, 1)

    sort(0, n)
    return pairs


SORT32 = batcher(32)


def exchange(x, pairs):
    for i, j in pairs:
        a, b = x[i], x[j]
        x[i] = jnp.maximum(a, b)
        x[j] = jnp.minimum(a, b)
    return x


def clean(x):
    d = len(x) // 2
    while d:
        exchange(x, [(i, i + d) for i in range(len(x)) if not i & d])
        d //= 2
    return x


MESH = pl.DeviceIdType.MESH


def route(n_cap, q_ref, probes_ref, send_ref, idx_ref):
    rows, width = q_ref.shape
    chunks, n_dev, chip_slots, _ = send_ref.shape
    chunk_slots = n_dev * chip_slots
    slots = chunks * chunk_slots
    each = chip_slots // n_cap
    n = lax.broadcasted_iota(jnp.int32, (slots, rows), 0)
    chip = (n % chunk_slots) // chip_slots
    part = chip * (chunks * each) + (n // chunk_slots) * each + (n % chip_slots) // n_cap
    rank_of = (n % n_cap).astype(jnp.float32)
    n_probe = probes_ref.shape[0]
    hits = [part == probes_ref[k : k + 1, :] for k in range(n_probe)]
    named = hits[0]
    for k in range(1, n_probe):
        named = named | hits[k]
    before = (
        lax.broadcasted_iota(jnp.int32, (rows, rows), 0) < lax.broadcasted_iota(jnp.int32, (rows, rows), 1)
    ).astype(jnp.float32).astype(jnp.bfloat16)
    rank = jnp.dot(named.astype(jnp.float32).astype(jnp.bfloat16), before, preferred_element_type=jnp.float32)
    chosen = named & (rank == rank_of)
    nf = jnp.where(chosen, n, 0)
    for k in range(n_probe):
        idx_ref[k : k + 1, :] = jnp.sum(jnp.where(hits[k], nf, 0), axis=0, keepdims=True)
    a = lax.broadcasted_iota(jnp.int32, (width, width), 0)
    b = lax.broadcasted_iota(jnp.int32, (width, width), 1)
    groups = width // 4
    j = (b >= groups).astype(jnp.int32) + (b >= 2 * groups).astype(jnp.int32) + (b >= 3 * groups).astype(jnp.int32)
    perm = jnp.where(a == (b - groups * j) * 4 + j, 1.0, 0.0).astype(jnp.bfloat16)
    moved = jnp.dot(q_ref[...], perm, preferred_element_type=jnp.float32).astype(jnp.bfloat16)
    pick = jnp.where(chosen, 1.0, 0.0).astype(jnp.bfloat16)
    picked = jnp.dot(pick, moved, preferred_element_type=jnp.float32)
    send_ref[...] = picked.astype(jnp.bfloat16).reshape(send_ref.shape)


def fill_table(book_ref, table_ref):
    n_cent, n_feat, groups = book_ref.shape
    for j in range(n_feat):
        plane = book_ref[:, j, :].astype(jnp.float32)
        wide = jnp.concatenate([plane, jnp.zeros((LANES - n_cent, groups), jnp.float32)], axis=0)
        table_ref[j] = wide.T


def decode(table_ref, codes_ref, p, t_ref, d_ref):
    groups, half = codes_ref.shape[1:]

    @pl.loop(0, groups // 16)
    def _(g):
        rows = pl.ds(pl.multiple_of(g * 16, 16), 16)
        tab = [table_ref[j, rows, :] for j in range(4)]
        for t in range(half // LANES):
            cols = slice(t * LANES, (t + 1) * LANES)
            c = codes_ref[p, rows, cols]
            for j in range(4):
                val = jnp.take_along_axis(tab[j], c, axis=1)
                t_ref[pl.ds(pl.multiple_of(j * groups + g * 16, 16), 16), cols] = val.astype(jnp.bfloat16)

    @pl.loop(0, half // 256)
    def _(t):
        cols = pl.ds(pl.multiple_of(t * 256, 256), 256)
        d_ref[p, cols, :] = t_ref[:, cols].T


def sort_block(s_ref, x_ref, b, dst):
    @pl.loop(0, 8)
    def _(g):
        x = exchange([s_ref[b, g * 32 + i] for i in range(32)], SORT32)
        for i in range(32):
            s_ref[b, g * 32 + i] = x[i]

    @pl.loop(0, 4)
    def _(g):
        base = g * 64
        high = clean([jnp.maximum(s_ref[b, base + i], s_ref[b, base + 63 - i]) for i in range(32)])
        low = clean([jnp.minimum(s_ref[b, base + i], s_ref[b, base + 63 - i]) for i in range(32)])
        for i in range(32):
            s_ref[b, base + i] = high[i]
            s_ref[b, base + 32 + i] = low[i]

    @pl.loop(0, 2)
    def _(g):
        base = g * 128
        for i in range(32):
            u0, u1 = s_ref[b, base + i], s_ref[b, base + 32 + i]
            v0, v1 = s_ref[b, base + 127 - i], s_ref[b, base + 95 - i]
            h0, h1 = jnp.maximum(u0, v0), jnp.maximum(u1, v1)
            l0, l1 = jnp.minimum(u0, v0), jnp.minimum(u1, v1)
            x_ref[dst, i] = jnp.maximum(h0, h1)
            x_ref[dst, 32 + i] = jnp.minimum(h0, h1)
            x_ref[dst, 64 + i] = jnp.maximum(l0, l1)
            x_ref[dst, 96 + i] = jnp.minimum(l0, l1)

        @pl.loop(0, 4, unroll=2)
        def _(k):
            x = clean([x_ref[dst, k * 32 + i] for i in range(32)])
            for i in range(32):
                s_ref[b, base + k * 32 + i] = x[i]

    for i in range(32):
        t = clean([jnp.maximum(s_ref[b, i + 32 * k], s_ref[b, 255 - i - 32 * k]) for k in range(4)])
        for k in range(4):
            x_ref[dst, i + 32 * k] = t[k]

    @pl.loop(0, 4, unroll=2)
    def _(k):
        x = clean([x_ref[dst, k * 32 + i] for i in range(32)])
        for i in range(32):
            x_ref[dst, k * 32 + i] = x[i]


def merge_pair(x_ref, y_ref, b0, b1, dst, level):
    bit = 1 << level
    sublane = lax.broadcasted_iota(jnp.int32, (SUBL, LANES), 0)
    lower = (sublane & bit) == 0
    for i in range(16):
        first, second = {}, {}
        for j in [i + 32 * k for k in range(4)] + [31 - i + 32 * k for k in range(4)]:
            p, q = x_ref[b0, j], x_ref[b1, j]
            first[j] = jnp.where(lower, p, q)
            second[j] = jnp.take_along_axis(jnp.where(lower, q, p), sublane ^ bit, axis=0)
        for r in (i, 31 - i):
            t = clean([jnp.maximum(first[r + 32 * k], second[127 - r - 32 * k]) for k in range(4)])
            for k in range(4):
                y_ref[r + 32 * k] = t[k]

    @pl.loop(0, 4, unroll=2)
    def _(k):
        x = clean([y_ref[k * 32 + i] for i in range(32)])
        for i in range(32):
            x_ref[dst, k * 32 + i] = x[i]


def kernel(
    n_cap, sizes_in, q_in, probes_in, book_in, codes_ref, out_ref,
    sizes_ref, q_ref, probes_ref, book_ref, send_ref, rows_ref, own_ref, t_ref, d_own, d_peer, table_ref,
    s_ref, x_ref, y_ref, z_ref, best_ref, back_ref, idx_ref,
    small_sem, in_sem, code_send, code_recv, row_send, row_recv, best_send, best_recv, row_keep, best_keep,
):
    chunks, n_dev, chip_slots, width = send_ref.shape
    part_dev, _, half = codes_ref.shape
    each = part_dev // chunks
    rep = lax.axis_index("rep")
    n_sub, n_dom = lax.axis_size("sub"), lax.axis_size("dom")
    my_dom, my_sub = lax.axis_index("dom"), lax.axis_index("sub")
    me = my_dom * n_sub + my_sub
    other = {"rep": 1 - rep}

    smalls = [
        pltpu.make_async_copy(src, dst, small_sem.at[i])
        for i, (src, dst) in enumerate(
            ((q_in, q_ref), (probes_in, probes_ref), (book_in, book_ref), (sizes_in, sizes_ref))
        )
    ]
    for c in smalls:
        c.start()
    loads = [pltpu.make_async_copy(codes_ref.at[p], own_ref.at[p], in_sem.at[p]) for p in range(part_dev)]
    for c in loads:
        c.start()
    barrier = pltpu.get_barrier_semaphore()
    pl.semaphore_signal(barrier, inc=1, device_id=other, device_id_type=MESH)

    def partners(visit):
        for ks in range(1, n_sub):
            visit(my_dom, lax.rem(my_sub + ks, n_sub))

        @pl.loop(1, n_dom)
        def _(kd):
            for ks in range(n_sub):
                visit(lax.rem(my_dom + kd, n_dom), lax.rem(my_sub + ks, n_sub))

    @partners
    def _(td, ts):
        pl.semaphore_signal(barrier, inc=1, device_id={"dom": td, "sub": ts}, device_id_type=MESH)

    for c in smalls:
        c.wait()
    route(n_cap, q_ref, probes_ref, send_ref, idx_ref)
    fill_table(book_ref, table_ref)
    pl.semaphore_wait(barrier, n_dev)

    def exchange_all(src, dst, send_sem, recv_sem, keep_sem):
        @partners
        def _(td, ts):
            pltpu.make_async_remote_copy(
                src_ref=src.at[td * n_sub + ts],
                dst_ref=dst.at[me],
                send_sem=send_sem,
                recv_sem=recv_sem,
                device_id={"dom": td, "sub": ts},
                device_id_type=MESH,
            ).start()

        pltpu.make_async_copy(src.at[me], dst.at[me], keep_sem).start()

    def finish_recv(src, dst, recv_sem, keep_sem):
        most = pl.ds(0, n_dev - 1)
        pltpu.make_async_copy(src.at[most], dst.at[most], recv_sem).wait()
        pltpu.make_async_copy(src.at[me], dst.at[me], keep_sem).wait()

    def finish_send(src, dst, send_sem):
        most = pl.ds(0, n_dev - 1)
        pltpu.make_async_copy(src.at[most], dst.at[most], send_sem).wait()

    swaps = [
        pltpu.make_async_remote_copy(
            src_ref=d_own.at[p],
            dst_ref=d_peer.at[p],
            send_sem=code_send.at[p],
            recv_sem=code_recv.at[p],
            device_id=other,
            device_id_type=MESH,
        )
        for p in range(part_dev)
    ]
    def send_rows(c):
        exchange_all(send_ref.at[c], rows_ref.at[c], row_send.at[c], row_recv.at[c], row_keep.at[c])

    send_rows(0)
    for p in range(part_dev):
        loads[p].wait()
        decode(table_ref, own_ref, p, t_ref, d_own)
        if p < each:
            swaps[p].start()
    send_rows(1)

    for c in range(chunks):
        finish_recv(send_ref.at[c], rows_ref.at[c], row_recv.at[c], row_keep.at[c])
        if c == 0:
            for p in range(each, part_dev):
                swaps[p].start()
        rows = rows_ref[c].reshape(n_dev * chip_slots, width)
        for e in range(each):
            p = c * each + e
            m = lax.broadcasted_iota(jnp.int32, (256, rows.shape[0]), 0)
            want = ((m // 128) * 32 + m % 32) * chip_slots + e * n_cap + (m % 128) // 32
            pick = jnp.where(lax.broadcasted_iota(jnp.int32, m.shape, 1) == want, 1.0, 0.0).astype(jnp.bfloat16)
            mine = jnp.dot(pick, rows, preferred_element_type=jnp.float32).astype(jnp.bfloat16)
            for which, ref in enumerate((d_own, d_peer)):
                if which == 1:
                    swaps[p].wait_recv()
                sc = lax.dot_general(ref[p], mine, (((1,), (1,)), ((), ())), preferred_element_type=jnp.float32)
                first = half * (rep if which == 0 else 1 - rep)
                ok = lax.broadcasted_iota(jnp.int32, (half, LANES), 0) + first < sizes_ref[p]
                for h in range(2):
                    blk = jnp.where(ok, sc[:, h * LANES : (h + 1) * LANES], MASKED)
                    s_ref[h, pl.ds(which * half // SUBL, half // SUBL)] = blk.reshape(half // SUBL, SUBL, LANES)

            @pl.loop(0, 2)
            def _(h):
                sort_block(s_ref, x_ref, h, e * 2 + h)

        @pl.loop(0, 2)
        def _(b):
            merge_pair(x_ref, y_ref, 2 * b, 2 * b + 1, b, 2)

        merge_pair(x_ref, y_ref, 0, 1, 0, 1)
        merge_pair(x_ref, y_ref, 0, 0, 0, 0)
        z_ref[...] = x_ref[0].reshape(RANKS * SUBL, LANES)
        for blk in range(4):
            u = 4 * (blk & 1) + (blk & 2)
            got = z_ref[pl.ds(u, RANKS, stride=SUBL), :].T
            for r in range(n_cap):
                slot = (blk >> 1) * n_cap + r
                best_ref[c, (blk & 1) * 32 : (blk & 1) * 32 + 32, slot, :] = got[r * 32 : (r + 1) * 32, :]
        exchange_all(best_ref.at[c], back_ref.at[c], best_send.at[c], best_recv.at[c], best_keep.at[c])

    found = None
    for c in range(chunks):
        finish_recv(best_ref.at[c], back_ref.at[c], best_recv.at[c], best_keep.at[c])
        got = select_lists(idx_ref, back_ref[c].reshape(n_dev * chip_slots, RANKS), c)
        found = got if found is None else found + got
    final_merge(found, out_ref)
    for c in range(chunks):
        finish_send(send_ref.at[c], rows_ref.at[c], row_send.at[c])
        finish_send(best_ref.at[c], back_ref.at[c], best_send.at[c])
    for c in swaps:
        c.wait_send()


def select_lists(idx_ref, lists, c):
    n_slots = lists.shape[0]
    wanted = jnp.concatenate([idx_ref[k : k + 1, :] for k in range(idx_ref.shape[0])], axis=1)
    slot = lax.broadcasted_iota(jnp.int32, (n_slots, wanted.shape[1]), 0) + c * n_slots
    pick = jnp.where(slot == wanted, 1.0, 0.0).astype(jnp.bfloat16)
    rest = lists.T
    parts = []
    for _ in range(3):
        part = rest.astype(jnp.bfloat16)
        rest = rest - part.astype(jnp.float32)
        parts.append(part)
    got = jnp.dot(jnp.concatenate(parts, axis=0), pick, preferred_element_type=jnp.float32)
    return got[:RANKS] + got[RANKS : 2 * RANKS] + got[2 * RANKS :]


def final_merge(x, out_ref):
    rows, n_out = out_ref.shape
    sublane = lax.broadcasted_iota(jnp.int32, (SUBL, LANES), 0)
    n_i = RANKS // SUBL
    cols = [
        [x[i * SUBL : (i + 1) * SUBL, t * LANES : (t + 1) * LANES] for i in range(n_i)]
        for t in range(x.shape[1] // LANES)
    ]

    def permuted(v, index):
        return jnp.take_along_axis(v, index, axis=0)

    def joined(a, b):
        m = clean([jnp.maximum(a[i], permuted(b[n_i - 1 - i], SUBL - 1 - sublane)) for i in range(n_i)])
        d = SUBL // 2
        while d:
            near = (sublane & d) == 0
            for i in range(n_i):
                other = permuted(m[i], sublane ^ d)
                m[i] = jnp.where(near, jnp.maximum(m[i], other), jnp.minimum(m[i], other))
            d //= 2
        return m

    while len(cols) > 1:
        h = len(cols) // 2
        cols = [joined(cols[t], cols[t + h]) for t in range(h)]
    m = cols[0]
    width = LANES
    while width > rows:
        width //= 2
        m = joined(m, [pltpu.roll(v, width, 1) for v in m])
    out_ref[...] = jnp.concatenate(m, axis=0).T[:rows, :n_out]


def local(queries, codebook, probes, codes, part_sizes):
    n_dev = lax.axis_size("dom") * lax.axis_size("sub")
    own_rows, width = queries.shape
    n_probe = probes.shape[1]
    part_dev, groups, half = codes.shape
    n_cap = max(2, 2 * own_rows * n_probe // (part_dev * n_dev))
    chunks = 2
    chip_slots = part_dev * n_cap // chunks
    book = codebook.transpose(1, 2, 0)
    args = [pltpu.with_memory_space_constraint(x, pltpu.HBM) for x in (part_sizes, queries, probes.T, book, codes)]
    hbm = pl.BlockSpec(memory_space=pltpu.HBM)
    vmem, dma = pltpu.VMEM, pltpu.SemaphoreType.DMA
    lists = vmem((chunks, n_dev, chip_slots, RANKS), jnp.float32)
    rows = vmem((chunks, n_dev, chip_slots, width), jnp.bfloat16)
    decoded = vmem((part_dev, half, width), jnp.bfloat16)
    return pl.pallas_call(
        functools.partial(kernel, n_cap),
        out_shape=jax.ShapeDtypeStruct((own_rows, TOPK), jnp.float32),
        in_specs=[hbm] * 5,
        out_specs=pl.BlockSpec(memory_space=pltpu.VMEM),
        scratch_shapes=[
            pltpu.SMEM(part_sizes.shape, jnp.int32),
            vmem(queries.shape, jnp.bfloat16),
            vmem((n_probe, own_rows), jnp.int32),
            vmem(book.shape, jnp.bfloat16),
            rows,
            rows,
            vmem(codes.shape, jnp.int32),
            vmem((width, half), jnp.bfloat16),
            decoded,
            decoded,
            vmem((book.shape[1], groups, LANES), jnp.float32),
            vmem((2, 2 * half // SUBL, SUBL, LANES), jnp.float32),
            vmem((4, RANKS, SUBL, LANES), jnp.float32),
            vmem((RANKS, SUBL, LANES), jnp.float32),
            vmem((RANKS * SUBL, LANES), jnp.float32),
            lists,
            lists,
            vmem((n_probe, own_rows), jnp.int32),
            dma((4,)),
            dma((part_dev,)),
            dma((part_dev,)),
            dma((part_dev,)),
            dma((chunks,)),
            dma((chunks,)),
            dma((chunks,)),
            dma((chunks,)),
            dma((chunks,)),
            dma((chunks,)),
        ],
        compiler_params=pltpu.CompilerParams(collective_id=0, has_side_effects=True, vmem_limit_bytes=40 << 20),
        name="search",
    )(*args)


def solution(mesh):
    in_specs = (
        P(("dom", "sub", "rep"), None),
        P(),
        P(("dom", "sub", "rep"), None),
        P(("dom", "sub"), None, "rep"),
        P(("dom", "sub")),
    )
    out_specs = P(("dom", "sub", "rep"), None)
    return jax.shard_map(local, mesh=mesh, in_specs=in_specs, out_specs=out_specs, check_vma=False)
```

```python
import functools

import jax
import jax.numpy as jnp
from jax import lax
from jax.experimental import pallas as pl
from jax.experimental.pallas import tpu as pltpu
from jax.sharding import PartitionSpec as P

TOPK = 100
MASKED = -1e30
RANKS = 128
LANES = 128
SUBL = 8


def batcher(n):
    pairs = []

    def merge(lo, cnt, r):
        step = r * 2
        if step < cnt:
            merge(lo, cnt, step)
            merge(lo + r, cnt, step)
            for i in range(lo + r, lo + cnt - r, step):
                pairs.append((i, i + r))
        else:
            pairs.append((lo, lo + r))

    def sort(lo, cnt):
        if cnt > 1:
            m = cnt // 2
            sort(lo, m)
            sort(lo + m, m)
            merge(lo, cnt, 1)

    sort(0, n)
    return pairs


SORT32 = batcher(32)


def exchange(x, pairs):
    for i, j in pairs:
        a, b = x[i], x[j]
        x[i] = jnp.maximum(a, b)
        x[j] = jnp.minimum(a, b)
    return x


def clean(x):
    d = len(x) // 2
    while d:
        exchange(x, [(i, i + d) for i in range(len(x)) if not i & d])
        d //= 2
    return x


MESH = pl.DeviceIdType.MESH


def route(n_cap, q_ref, probes_ref, send_ref, idx_ref):
    rows, width = q_ref.shape
    chunks, n_dev, chip_slots, _ = send_ref.shape
    chunk_slots = n_dev * chip_slots
    slots = chunks * chunk_slots
    each = chip_slots // n_cap
    n = lax.broadcasted_iota(jnp.int32, (slots, rows), 0)
    chip = (n % chunk_slots) // chip_slots
    part = chip * (chunks * each) + (n // chunk_slots) * each + (n % chip_slots) // n_cap
    rank_of = (n % n_cap).astype(jnp.float32)
    n_probe = probes_ref.shape[0]
    hits = [part == probes_ref[k : k + 1, :] for k in range(n_probe)]
    named = hits[0]
    for k in range(1, n_probe):
        named = named | hits[k]
    before = (
        lax.broadcasted_iota(jnp.int32, (rows, rows), 0) < lax.broadcasted_iota(jnp.int32, (rows, rows), 1)
    ).astype(jnp.float32).astype(jnp.bfloat16)
    rank = jnp.dot(named.astype(jnp.float32).astype(jnp.bfloat16), before, preferred_element_type=jnp.float32)
    chosen = named & (rank == rank_of)
    nf = jnp.where(chosen, n, 0)
    for k in range(n_probe):
        idx_ref[k : k + 1, :] = jnp.sum(jnp.where(hits[k], nf, 0), axis=0, keepdims=True)
    a = lax.broadcasted_iota(jnp.int32, (width, width), 0)
    b = lax.broadcasted_iota(jnp.int32, (width, width), 1)
    groups = width // 4
    j = (b >= groups).astype(jnp.int32) + (b >= 2 * groups).astype(jnp.int32) + (b >= 3 * groups).astype(jnp.int32)
    perm = jnp.where(a == (b - groups * j) * 4 + j, 1.0, 0.0).astype(jnp.bfloat16)
    moved = jnp.dot(q_ref[...], perm, preferred_element_type=jnp.float32).astype(jnp.bfloat16)
    pick = jnp.where(chosen, 1.0, 0.0).astype(jnp.bfloat16)
    picked = jnp.dot(pick, moved, preferred_element_type=jnp.float32)
    send_ref[...] = picked.astype(jnp.bfloat16).reshape(send_ref.shape)


def fill_table(book_ref, table_ref):
    n_cent, n_feat, groups = book_ref.shape
    for j in range(n_feat):
        plane = book_ref[:, j, :].astype(jnp.float32)
        wide = jnp.concatenate([plane, jnp.zeros((LANES - n_cent, groups), jnp.float32)], axis=0)
        table_ref[j] = wide.T


def decode(table_ref, codes_ref, p, t_ref, d_ref):
    groups, half = codes_ref.shape[1:]

    @pl.loop(0, groups // 16)
    def _(g):
        rows = pl.ds(pl.multiple_of(g * 16, 16), 16)
        tab = [table_ref[j, rows, :] for j in range(4)]
        for t in range(half // LANES):
            cols = slice(t * LANES, (t + 1) * LANES)
            c = codes_ref[p, rows, cols]
            for j in range(4):
                val = jnp.take_along_axis(tab[j], c, axis=1)
                t_ref[pl.ds(pl.multiple_of(j * groups + g * 16, 16), 16), cols] = val.astype(jnp.bfloat16)

    @pl.loop(0, half // 256)
    def _(t):
        cols = pl.ds(pl.multiple_of(t * 256, 256), 256)
        d_ref[p, cols, :] = t_ref[:, cols].T


def sort_half(s_ref, x_ref, b, start):
    @pl.loop(0, 4)
    def _(g):
        base = start + g * 32
        x = exchange([s_ref[b, base + i] for i in range(32)], SORT32)
        for i in range(32):
            s_ref[b, base + i] = x[i]

    @pl.loop(0, 2)
    def _(g):
        base = start + g * 64
        high = clean([jnp.maximum(s_ref[b, base + i], s_ref[b, base + 63 - i]) for i in range(32)])
        low = clean([jnp.minimum(s_ref[b, base + i], s_ref[b, base + 63 - i]) for i in range(32)])
        for i in range(32):
            s_ref[b, base + i] = high[i]
            s_ref[b, base + 32 + i] = low[i]

    for i in range(32):
        u0, u1 = s_ref[b, start + i], s_ref[b, start + 32 + i]
        v0, v1 = s_ref[b, start + 127 - i], s_ref[b, start + 95 - i]
        h0, h1 = jnp.maximum(u0, v0), jnp.maximum(u1, v1)
        l0, l1 = jnp.minimum(u0, v0), jnp.minimum(u1, v1)
        x_ref[b, i] = jnp.maximum(h0, h1)
        x_ref[b, 32 + i] = jnp.minimum(h0, h1)
        x_ref[b, 64 + i] = jnp.maximum(l0, l1)
        x_ref[b, 96 + i] = jnp.minimum(l0, l1)

    @pl.loop(0, 4, unroll=2)
    def _(k):
        x = clean([x_ref[b, k * 32 + i] for i in range(32)])
        for i in range(32):
            s_ref[b, start + k * 32 + i] = x[i]


def join_halves(s_ref, x_ref, b):
    for i in range(32):
        t = clean([jnp.maximum(s_ref[b, i + 32 * k], s_ref[b, 255 - i - 32 * k]) for k in range(4)])
        for k in range(4):
            x_ref[b, i + 32 * k] = t[k]

    @pl.loop(0, 4, unroll=2)
    def _(k):
        x = clean([x_ref[b, k * 32 + i] for i in range(32)])
        for i in range(32):
            x_ref[b, k * 32 + i] = x[i]


def merge_pair(x_ref, y_ref, b0, b1, dst, level):
    bit = 1 << level
    sublane = lax.broadcasted_iota(jnp.int32, (SUBL, LANES), 0)
    lower = (sublane & bit) == 0
    for i in range(16):
        first, second = {}, {}
        for j in [i + 32 * k for k in range(4)] + [31 - i + 32 * k for k in range(4)]:
            p, q = x_ref[b0, j], x_ref[b1, j]
            first[j] = jnp.where(lower, p, q)
            second[j] = jnp.take_along_axis(jnp.where(lower, q, p), sublane ^ bit, axis=0)
        for r in (i, 31 - i):
            t = clean([jnp.maximum(first[r + 32 * k], second[127 - r - 32 * k]) for k in range(4)])
            for k in range(4):
                y_ref[r + 32 * k] = t[k]

    @pl.loop(0, 4, unroll=2)
    def _(k):
        x = clean([y_ref[k * 32 + i] for i in range(32)])
        for i in range(32):
            x_ref[dst, k * 32 + i] = x[i]


def kernel(
    n_cap, sizes_in, q_in, probes_in, book_in, codes_ref, out_ref,
    sizes_ref, q_ref, probes_ref, book_ref, send_ref, rows_ref, own_ref, t_ref, d_own, d_peer, table_ref,
    mine_ref, s_ref, x_ref, y_ref, z_ref, best_ref, back_ref, idx_ref,
    small_sem, in_sem, code_send, code_recv, row_send, row_recv, best_send, best_recv, row_keep, best_keep,
):
    chunks, n_dev, chip_slots, width = send_ref.shape
    part_dev, _, half = codes_ref.shape
    each = part_dev // chunks
    rep = lax.axis_index("rep")
    n_sub, n_dom = lax.axis_size("sub"), lax.axis_size("dom")
    my_dom, my_sub = lax.axis_index("dom"), lax.axis_index("sub")
    me = my_dom * n_sub + my_sub
    other = {"rep": 1 - rep}

    smalls = [
        pltpu.make_async_copy(src, dst, small_sem.at[i])
        for i, (src, dst) in enumerate(
            ((q_in, q_ref), (probes_in, probes_ref), (book_in, book_ref), (sizes_in, sizes_ref))
        )
    ]
    for c in smalls:
        c.start()
    loads = [pltpu.make_async_copy(codes_ref.at[p], own_ref.at[p], in_sem.at[p]) for p in range(part_dev)]
    for c in loads:
        c.start()
    barrier = pltpu.get_barrier_semaphore()
    pl.semaphore_signal(barrier, inc=1, device_id=other, device_id_type=MESH)

    def partners(visit):
        for ks in range(1, n_sub):
            visit(my_dom, lax.rem(my_sub + ks, n_sub))

        @pl.loop(1, n_dom)
        def _(kd):
            for ks in range(n_sub):
                visit(lax.rem(my_dom + kd, n_dom), lax.rem(my_sub + ks, n_sub))

    @partners
    def _(td, ts):
        pl.semaphore_signal(barrier, inc=1, device_id={"dom": td, "sub": ts}, device_id_type=MESH)

    for c in smalls:
        c.wait()
    route(n_cap, q_ref, probes_ref, send_ref, idx_ref)
    fill_table(book_ref, table_ref)
    pl.semaphore_wait(barrier, n_dev)

    def exchange_all(src, dst, send_sem, recv_sem, keep_sem):
        @partners
        def _(td, ts):
            pltpu.make_async_remote_copy(
                src_ref=src.at[td * n_sub + ts],
                dst_ref=dst.at[me],
                send_sem=send_sem,
                recv_sem=recv_sem,
                device_id={"dom": td, "sub": ts},
                device_id_type=MESH,
            ).start()

        pltpu.make_async_copy(src.at[me], dst.at[me], keep_sem).start()

    def finish_recv(src, dst, recv_sem, keep_sem):
        most = pl.ds(0, n_dev - 1)
        pltpu.make_async_copy(src.at[most], dst.at[most], recv_sem).wait()
        pltpu.make_async_copy(src.at[me], dst.at[me], keep_sem).wait()

    def finish_send(src, dst, send_sem):
        most = pl.ds(0, n_dev - 1)
        pltpu.make_async_copy(src.at[most], dst.at[most], send_sem).wait()

    swaps = [
        pltpu.make_async_remote_copy(
            src_ref=d_own.at[p],
            dst_ref=d_peer.at[p],
            send_sem=code_send.at[p],
            recv_sem=code_recv.at[p],
            device_id=other,
            device_id_type=MESH,
        )
        for p in range(part_dev)
    ]
    def send_rows(c):
        exchange_all(send_ref.at[c], rows_ref.at[c], row_send.at[c], row_recv.at[c], row_keep.at[c])

    send_rows(0)
    for p in range(part_dev):
        loads[p].wait()
        decode(table_ref, own_ref, p, t_ref, d_own)
        if p < each:
            swaps[p].start()
    send_rows(1)

    for c in range(chunks):
        finish_recv(send_ref.at[c], rows_ref.at[c], row_recv.at[c], row_keep.at[c])
        if c == 0:
            for p in range(each, part_dev):
                swaps[p].start()
        rows = rows_ref[c].reshape(n_dev * chip_slots, width)
        n_half = half // SUBL
        for e in range(each):
            m = lax.broadcasted_iota(jnp.int32, (256, rows.shape[0]), 0)
            want = ((m // 128) * 32 + m % 32) * chip_slots + e * n_cap + (m % 128) // 32
            pick = jnp.where(lax.broadcasted_iota(jnp.int32, m.shape, 1) == want, 1.0, 0.0).astype(jnp.bfloat16)
            mine_ref[e] = jnp.dot(pick, rows, preferred_element_type=jnp.float32).astype(jnp.bfloat16)
        for which, ref in enumerate((d_own, d_peer)):
            first = half * (rep if which == 0 else 1 - rep)
            for e in range(each):
                p = c * each + e
                if which == 1:
                    swaps[p].wait_recv()
                sc = lax.dot_general(
                    ref[p], mine_ref[e], (((1,), (1,)), ((), ())), preferred_element_type=jnp.float32
                )
                ok = lax.broadcasted_iota(jnp.int32, (half, LANES), 0) + first < sizes_ref[p]
                for h in range(2):
                    blk = jnp.where(ok, sc[:, h * LANES : (h + 1) * LANES], MASKED)
                    s_ref[e * 2 + h, pl.ds(which * n_half, n_half)] = blk.reshape(n_half, SUBL, LANES)

            @pl.loop(0, 2 * each)
            def _(b):
                sort_half(s_ref, x_ref, b, which * n_half)

        @pl.loop(0, 2 * each)
        def _(b):
            join_halves(s_ref, x_ref, b)

        @pl.loop(0, 2)
        def _(b):
            merge_pair(x_ref, y_ref, 2 * b, 2 * b + 1, b, 2)

        merge_pair(x_ref, y_ref, 0, 1, 0, 1)
        merge_pair(x_ref, y_ref, 0, 0, 0, 0)
        z_ref[...] = x_ref[0].reshape(RANKS * SUBL, LANES)
        for blk in range(4):
            u = 4 * (blk & 1) + (blk & 2)
            got = z_ref[pl.ds(u, RANKS, stride=SUBL), :].T
            for r in range(n_cap):
                slot = (blk >> 1) * n_cap + r
                best_ref[c, (blk & 1) * 32 : (blk & 1) * 32 + 32, slot, :] = got[r * 32 : (r + 1) * 32, :]
        exchange_all(best_ref.at[c], back_ref.at[c], best_send.at[c], best_recv.at[c], best_keep.at[c])

    found = None
    for c in range(chunks):
        finish_recv(best_ref.at[c], back_ref.at[c], best_recv.at[c], best_keep.at[c])
        got = select_lists(idx_ref, back_ref[c].reshape(n_dev * chip_slots, RANKS), c)
        found = got if found is None else found + got
    final_merge(found, out_ref)
    for c in range(chunks):
        finish_send(send_ref.at[c], rows_ref.at[c], row_send.at[c])
        finish_send(best_ref.at[c], back_ref.at[c], best_send.at[c])
    for c in swaps:
        c.wait_send()


def select_lists(idx_ref, lists, c):
    n_slots = lists.shape[0]
    wanted = jnp.concatenate([idx_ref[k : k + 1, :] for k in range(idx_ref.shape[0])], axis=1)
    slot = lax.broadcasted_iota(jnp.int32, (n_slots, wanted.shape[1]), 0) + c * n_slots
    pick = jnp.where(slot == wanted, 1.0, 0.0).astype(jnp.bfloat16)
    rest = lists.T
    parts = []
    for _ in range(3):
        part = rest.astype(jnp.bfloat16)
        rest = rest - part.astype(jnp.float32)
        parts.append(part)
    got = jnp.dot(jnp.concatenate(parts, axis=0), pick, preferred_element_type=jnp.float32)
    return got[:RANKS] + got[RANKS : 2 * RANKS] + got[2 * RANKS :]


def final_merge(x, out_ref):
    rows, n_out = out_ref.shape
    sublane = lax.broadcasted_iota(jnp.int32, (SUBL, LANES), 0)
    n_i = RANKS // SUBL
    cols = [
        [x[i * SUBL : (i + 1) * SUBL, t * LANES : (t + 1) * LANES] for i in range(n_i)]
        for t in range(x.shape[1] // LANES)
    ]

    def permuted(v, index):
        return jnp.take_along_axis(v, index, axis=0)

    def joined(a, b):
        m = clean([jnp.maximum(a[i], permuted(b[n_i - 1 - i], SUBL - 1 - sublane)) for i in range(n_i)])
        d = SUBL // 2
        while d:
            near = (sublane & d) == 0
            for i in range(n_i):
                other = permuted(m[i], sublane ^ d)
                m[i] = jnp.where(near, jnp.maximum(m[i], other), jnp.minimum(m[i], other))
            d //= 2
        return m

    while len(cols) > 1:
        h = len(cols) // 2
        cols = [joined(cols[t], cols[t + h]) for t in range(h)]
    m = cols[0]
    width = LANES
    while width > rows:
        width //= 2
        m = joined(m, [pltpu.roll(v, width, 1) for v in m])
    out_ref[...] = jnp.concatenate(m, axis=0).T[:rows, :n_out]


def local(queries, codebook, probes, codes, part_sizes):
    n_dev = lax.axis_size("dom") * lax.axis_size("sub")
    own_rows, width = queries.shape
    n_probe = probes.shape[1]
    part_dev, groups, half = codes.shape
    n_cap = max(2, 2 * own_rows * n_probe // (part_dev * n_dev))
    chunks = 2
    chip_slots = part_dev * n_cap // chunks
    book = codebook.transpose(1, 2, 0)
    args = [pltpu.with_memory_space_constraint(x, pltpu.HBM) for x in (part_sizes, queries, probes.T, book, codes)]
    hbm = pl.BlockSpec(memory_space=pltpu.HBM)
    vmem, dma = pltpu.VMEM, pltpu.SemaphoreType.DMA
    lists = vmem((chunks, n_dev, chip_slots, RANKS), jnp.float32)
    rows = vmem((chunks, n_dev, chip_slots, width), jnp.bfloat16)
    decoded = vmem((part_dev, half, width), jnp.bfloat16)
    return pl.pallas_call(
        functools.partial(kernel, n_cap),
        out_shape=jax.ShapeDtypeStruct((own_rows, TOPK), jnp.float32),
        in_specs=[hbm] * 5,
        out_specs=pl.BlockSpec(memory_space=pltpu.VMEM),
        scratch_shapes=[
            pltpu.SMEM(part_sizes.shape, jnp.int32),
            vmem(queries.shape, jnp.bfloat16),
            vmem((n_probe, own_rows), jnp.int32),
            vmem(book.shape, jnp.bfloat16),
            rows,
            rows,
            vmem(codes.shape, jnp.int32),
            vmem((width, half), jnp.bfloat16),
            decoded,
            decoded,
            vmem((book.shape[1], groups, LANES), jnp.float32),
            vmem((2, 256, width), jnp.bfloat16),
            vmem((4, 2 * half // SUBL, SUBL, LANES), jnp.float32),
            vmem((4, RANKS, SUBL, LANES), jnp.float32),
            vmem((RANKS, SUBL, LANES), jnp.float32),
            vmem((RANKS * SUBL, LANES), jnp.float32),
            lists,
            lists,
            vmem((n_probe, own_rows), jnp.int32),
            dma((4,)),
            dma((part_dev,)),
            dma((part_dev,)),
            dma((part_dev,)),
            dma((chunks,)),
            dma((chunks,)),
            dma((chunks,)),
            dma((chunks,)),
            dma((chunks,)),
            dma((chunks,)),
        ],
        compiler_params=pltpu.CompilerParams(collective_id=0, has_side_effects=True, vmem_limit_bytes=40 << 20),
        name="search",
    )(*args)


def solution(mesh):
    in_specs = (
        P(("dom", "sub", "rep"), None),
        P(),
        P(("dom", "sub", "rep"), None),
        P(("dom", "sub"), None, "rep"),
        P(("dom", "sub")),
    )
    out_specs = P(("dom", "sub", "rep"), None)
    return jax.shard_map(local, mesh=mesh, in_specs=in_specs, out_specs=out_specs, check_vma=False)
```

```python
import functools

import jax
import jax.numpy as jnp
from jax import lax
from jax.experimental import pallas as pl
from jax.experimental.pallas import tpu as pltpu
from jax.sharding import PartitionSpec as P

TOPK = 100
MASKED = -1e30
RANKS = 128
LANES = 128
SUBL = 8


def batcher(n):
    pairs = []

    def merge(lo, cnt, r):
        step = r * 2
        if step < cnt:
            merge(lo, cnt, step)
            merge(lo + r, cnt, step)
            for i in range(lo + r, lo + cnt - r, step):
                pairs.append((i, i + r))
        else:
            pairs.append((lo, lo + r))

    def sort(lo, cnt):
        if cnt > 1:
            m = cnt // 2
            sort(lo, m)
            sort(lo + m, m)
            merge(lo, cnt, 1)

    sort(0, n)
    return pairs


SORT32 = batcher(32)


def exchange(x, pairs):
    for i, j in pairs:
        a, b = x[i], x[j]
        x[i] = jnp.maximum(a, b)
        x[j] = jnp.minimum(a, b)
    return x


def clean(x):
    d = len(x) // 2
    while d:
        exchange(x, [(i, i + d) for i in range(len(x)) if not i & d])
        d //= 2
    return x


MESH = pl.DeviceIdType.MESH


def route(n_cap, q_ref, probes_ref, send_ref, idx_ref):
    rows, width = q_ref.shape
    chunks, n_dev, chip_slots, _ = send_ref.shape
    chunk_slots = n_dev * chip_slots
    slots = chunks * chunk_slots
    each = chip_slots // n_cap
    n = lax.broadcasted_iota(jnp.int32, (slots, rows), 0)
    chip = (n % chunk_slots) // chip_slots
    part = chip * (chunks * each) + (n // chunk_slots) * each + (n % chip_slots) // n_cap
    rank_of = (n % n_cap).astype(jnp.float32)
    n_probe = probes_ref.shape[0]
    hits = [part == probes_ref[k : k + 1, :] for k in range(n_probe)]
    named = hits[0]
    for k in range(1, n_probe):
        named = named | hits[k]
    before = (
        lax.broadcasted_iota(jnp.int32, (rows, rows), 0) < lax.broadcasted_iota(jnp.int32, (rows, rows), 1)
    ).astype(jnp.float32).astype(jnp.bfloat16)
    rank = jnp.dot(named.astype(jnp.float32).astype(jnp.bfloat16), before, preferred_element_type=jnp.float32)
    chosen = named & (rank == rank_of)
    nf = jnp.where(chosen, n, 0)
    for k in range(n_probe):
        idx_ref[k : k + 1, :] = jnp.sum(jnp.where(hits[k], nf, 0), axis=0, keepdims=True)
    a = lax.broadcasted_iota(jnp.int32, (width, width), 0)
    b = lax.broadcasted_iota(jnp.int32, (width, width), 1)
    groups = width // 4
    j = (b >= groups).astype(jnp.int32) + (b >= 2 * groups).astype(jnp.int32) + (b >= 3 * groups).astype(jnp.int32)
    perm = jnp.where(a == (b - groups * j) * 4 + j, 1.0, 0.0).astype(jnp.bfloat16)
    moved = jnp.dot(q_ref[...], perm, preferred_element_type=jnp.float32).astype(jnp.bfloat16)
    pick = jnp.where(chosen, 1.0, 0.0).astype(jnp.bfloat16)
    picked = jnp.dot(pick, moved, preferred_element_type=jnp.float32)
    send_ref[...] = picked.astype(jnp.bfloat16).reshape(send_ref.shape)


def fill_table(book_ref, table_ref):
    n_cent, n_feat, groups = book_ref.shape
    for j in range(n_feat):
        plane = book_ref[:, j, :].astype(jnp.float32)
        wide = jnp.concatenate([plane, jnp.zeros((LANES - n_cent, groups), jnp.float32)], axis=0)
        table_ref[j] = wide.T


def decode(table_ref, codes_ref, p, t_ref, d_ref):
    groups, half = codes_ref.shape[1:]

    @pl.loop(0, groups // 16)
    def _(g):
        rows = pl.ds(pl.multiple_of(g * 16, 16), 16)
        tab = [table_ref[j, rows, :] for j in range(4)]
        for t in range(half // LANES):
            cols = slice(t * LANES, (t + 1) * LANES)
            c = codes_ref[p, rows, cols]
            for j in range(4):
                val = jnp.take_along_axis(tab[j], c, axis=1)
                t_ref[pl.ds(pl.multiple_of(j * groups + g * 16, 16), 16), cols] = val.astype(jnp.bfloat16)

    @pl.loop(0, half // 256)
    def _(t):
        cols = pl.ds(pl.multiple_of(t * 256, 256), 256)
        d_ref[p, cols, :] = t_ref[:, cols].T


def sort_half(s_ref, x_ref, b, start):
    @pl.loop(0, 4)
    def _(g):
        base = start + g * 32
        x = exchange([s_ref[b, base + i] for i in range(32)], SORT32)
        for i in range(32):
            s_ref[b, base + i] = x[i]

    @pl.loop(0, 2)
    def _(g):
        base = start + g * 64
        high = clean([jnp.maximum(s_ref[b, base + i], s_ref[b, base + 63 - i]) for i in range(32)])
        low = clean([jnp.minimum(s_ref[b, base + i], s_ref[b, base + 63 - i]) for i in range(32)])
        for i in range(32):
            s_ref[b, base + i] = high[i]
            s_ref[b, base + 32 + i] = low[i]

    for i in range(32):
        u0, u1 = s_ref[b, start + i], s_ref[b, start + 32 + i]
        v0, v1 = s_ref[b, start + 127 - i], s_ref[b, start + 95 - i]
        h0, h1 = jnp.maximum(u0, v0), jnp.maximum(u1, v1)
        l0, l1 = jnp.minimum(u0, v0), jnp.minimum(u1, v1)
        x_ref[b, i] = jnp.maximum(h0, h1)
        x_ref[b, 32 + i] = jnp.minimum(h0, h1)
        x_ref[b, 64 + i] = jnp.maximum(l0, l1)
        x_ref[b, 96 + i] = jnp.minimum(l0, l1)

    @pl.loop(0, 4, unroll=2)
    def _(k):
        x = clean([x_ref[b, k * 32 + i] for i in range(32)])
        for i in range(32):
            s_ref[b, start + k * 32 + i] = x[i]


def join_halves(s_ref, x_ref, b):
    for i in range(32):
        t = clean([jnp.maximum(s_ref[b, i + 32 * k], s_ref[b, 255 - i - 32 * k]) for k in range(4)])
        for k in range(4):
            x_ref[b, i + 32 * k] = t[k]

    @pl.loop(0, 4, unroll=2)
    def _(k):
        x = clean([x_ref[b, k * 32 + i] for i in range(32)])
        for i in range(32):
            x_ref[b, k * 32 + i] = x[i]


def merge_pair(x_ref, y_ref, b0, b1, dst, level):
    bit = 1 << level
    sublane = lax.broadcasted_iota(jnp.int32, (SUBL, LANES), 0)
    lower = (sublane & bit) == 0
    for i in range(16):
        first, second = {}, {}
        for j in [i + 32 * k for k in range(4)] + [31 - i + 32 * k for k in range(4)]:
            p, q = x_ref[b0, j], x_ref[b1, j]
            first[j] = jnp.where(lower, p, q)
            second[j] = jnp.take_along_axis(jnp.where(lower, q, p), sublane ^ bit, axis=0)
        for r in (i, 31 - i):
            t = clean([jnp.maximum(first[r + 32 * k], second[127 - r - 32 * k]) for k in range(4)])
            for k in range(4):
                y_ref[r + 32 * k] = t[k]

    @pl.loop(0, 4, unroll=2)
    def _(k):
        x = clean([y_ref[k * 32 + i] for i in range(32)])
        for i in range(32):
            x_ref[dst, k * 32 + i] = x[i]


def kernel(
    n_cap, sizes_in, q_in, probes_in, book_in, codes_ref, out_ref,
    sizes_ref, q_ref, probes_ref, book_ref, send_ref, rows_ref, own_ref, t_ref, d_own, d_peer, table_ref,
    pick_ref, choice_ref, mine_ref, s_ref, x_ref, y_ref, z_ref, best_ref, back_ref, idx_ref,
    small_sem, in_sem, code_send, code_recv, row_send, row_recv, best_send, best_recv, row_keep, best_keep,
):
    chunks, n_dev, chip_slots, width = send_ref.shape
    part_dev, _, half = codes_ref.shape
    each = part_dev // chunks
    rep = lax.axis_index("rep")
    n_sub, n_dom = lax.axis_size("sub"), lax.axis_size("dom")
    my_dom, my_sub = lax.axis_index("dom"), lax.axis_index("sub")
    me = my_dom * n_sub + my_sub
    other = {"rep": 1 - rep}

    smalls = [
        pltpu.make_async_copy(src, dst, small_sem.at[i])
        for i, (src, dst) in enumerate(
            ((q_in, q_ref), (probes_in, probes_ref), (book_in, book_ref), (sizes_in, sizes_ref))
        )
    ]
    for c in smalls:
        c.start()
    loads = [pltpu.make_async_copy(codes_ref.at[p], own_ref.at[p], in_sem.at[p]) for p in range(part_dev)]
    for c in loads:
        c.start()
    barrier = pltpu.get_barrier_semaphore()
    pl.semaphore_signal(barrier, inc=1, device_id=other, device_id_type=MESH)

    def partners(visit):
        for ks in range(1, n_sub):
            visit(my_dom, lax.rem(my_sub + ks, n_sub))

        @pl.loop(1, n_dom)
        def _(kd):
            for ks in range(n_sub):
                visit(lax.rem(my_dom + kd, n_dom), lax.rem(my_sub + ks, n_sub))

    @partners
    def _(td, ts):
        pl.semaphore_signal(barrier, inc=1, device_id={"dom": td, "sub": ts}, device_id_type=MESH)

    for c in smalls:
        c.wait()
    route(n_cap, q_ref, probes_ref, send_ref, idx_ref)
    fill_table(book_ref, table_ref)
    pl.semaphore_wait(barrier, n_dev)

    def exchange_all(src, dst, send_sem, recv_sem, keep_sem):
        @partners
        def _(td, ts):
            pltpu.make_async_remote_copy(
                src_ref=src.at[td * n_sub + ts],
                dst_ref=dst.at[me],
                send_sem=send_sem,
                recv_sem=recv_sem,
                device_id={"dom": td, "sub": ts},
                device_id_type=MESH,
            ).start()

        pltpu.make_async_copy(src.at[me], dst.at[me], keep_sem).start()

    def finish_recv(src, dst, recv_sem, keep_sem):
        most = pl.ds(0, n_dev - 1)
        pltpu.make_async_copy(src.at[most], dst.at[most], recv_sem).wait()
        pltpu.make_async_copy(src.at[me], dst.at[me], keep_sem).wait()

    def finish_send(src, dst, send_sem):
        most = pl.ds(0, n_dev - 1)
        pltpu.make_async_copy(src.at[most], dst.at[most], send_sem).wait()

    swaps = [
        pltpu.make_async_remote_copy(
            src_ref=d_own.at[p],
            dst_ref=d_peer.at[p],
            send_sem=code_send.at[p],
            recv_sem=code_recv.at[p],
            device_id=other,
            device_id_type=MESH,
        )
        for p in range(part_dev)
    ]
    def send_rows(c):
        exchange_all(send_ref.at[c], rows_ref.at[c], row_send.at[c], row_recv.at[c], row_keep.at[c])

    send_rows(0)
    for p in range(part_dev):
        loads[p].wait()
        decode(table_ref, own_ref, p, t_ref, d_own)
        if p < each:
            swaps[p].start()
    send_rows(1)
    for e in range(each):
        m = lax.broadcasted_iota(jnp.int32, pick_ref.shape[1:], 0)
        want = ((m // 128) * 32 + m % 32) * chip_slots + e * n_cap + (m % 128) // 32
        here = lax.broadcasted_iota(jnp.int32, m.shape, 1)
        pick_ref[e] = jnp.where(here == want, 1.0, 0.0).astype(jnp.bfloat16)
    fill_choice(idx_ref, choice_ref)

    for c in range(chunks):
        finish_recv(send_ref.at[c], rows_ref.at[c], row_recv.at[c], row_keep.at[c])
        if c == 0:
            for p in range(each, part_dev):
                swaps[p].start()
        rows = rows_ref[c].reshape(n_dev * chip_slots, width)
        n_half = half // SUBL
        for e in range(each):
            mine_ref[e] = jnp.dot(pick_ref[e], rows, preferred_element_type=jnp.float32).astype(jnp.bfloat16)
        for which, ref in enumerate((d_own, d_peer)):
            first = half * (rep if which == 0 else 1 - rep)
            for e in range(each):
                p = c * each + e
                if which == 1:
                    swaps[p].wait_recv()
                sc = lax.dot_general(
                    ref[p], mine_ref[e], (((1,), (1,)), ((), ())), preferred_element_type=jnp.float32
                )
                ok = lax.broadcasted_iota(jnp.int32, (half, LANES), 0) + first < sizes_ref[p]
                for h in range(2):
                    blk = jnp.where(ok, sc[:, h * LANES : (h + 1) * LANES], MASKED)
                    s_ref[e * 2 + h, pl.ds(which * n_half, n_half)] = blk.reshape(n_half, SUBL, LANES)

            @pl.loop(0, 2 * each)
            def _(b):
                sort_half(s_ref, x_ref, b, which * n_half)

        @pl.loop(0, 2 * each)
        def _(b):
            join_halves(s_ref, x_ref, b)

        @pl.loop(0, 2)
        def _(b):
            merge_pair(x_ref, y_ref, 2 * b, 2 * b + 1, b, 2)

        merge_pair(x_ref, y_ref, 0, 1, 0, 1)
        merge_pair(x_ref, y_ref, 0, 0, 0, 0)
        z_ref[...] = x_ref[0].reshape(RANKS * SUBL, LANES)
        for blk in range(4):
            u = 4 * (blk & 1) + (blk & 2)
            got = z_ref[pl.ds(u, RANKS, stride=SUBL), :].T
            for r in range(n_cap):
                slot = (blk >> 1) * n_cap + r
                best_ref[c, (blk & 1) * 32 : (blk & 1) * 32 + 32, slot, :] = got[r * 32 : (r + 1) * 32, :]
        exchange_all(best_ref.at[c], back_ref.at[c], best_send.at[c], best_recv.at[c], best_keep.at[c])

    found = None
    for c in range(chunks):
        finish_recv(best_ref.at[c], back_ref.at[c], best_recv.at[c], best_keep.at[c])
        got = select_lists(choice_ref[c], back_ref[c].reshape(n_dev * chip_slots, RANKS))
        found = got if found is None else found + got
    final_merge(found, out_ref)
    for c in range(chunks):
        finish_send(send_ref.at[c], rows_ref.at[c], row_send.at[c])
        finish_send(best_ref.at[c], back_ref.at[c], best_send.at[c])
    for c in swaps:
        c.wait_send()


def fill_choice(idx_ref, choice_ref):
    chunks, n_slots, n_lists = choice_ref.shape
    wanted = jnp.concatenate([idx_ref[k : k + 1, :] for k in range(idx_ref.shape[0])], axis=1)
    slot = lax.broadcasted_iota(jnp.int32, (n_slots, n_lists), 0)
    for c in range(chunks):
        choice_ref[c] = jnp.where(slot == wanted - c * n_slots, 1.0, 0.0).astype(jnp.bfloat16)


def select_lists(choice, lists):
    rest = lists.T
    parts = []
    for _ in range(3):
        part = rest.astype(jnp.bfloat16)
        rest = rest - part.astype(jnp.float32)
        parts.append(part)
    got = jnp.dot(jnp.concatenate(parts, axis=0), choice, preferred_element_type=jnp.float32)
    return got[:RANKS] + got[RANKS : 2 * RANKS] + got[2 * RANKS :]


def final_merge(x, out_ref):
    rows, n_out = out_ref.shape
    sublane = lax.broadcasted_iota(jnp.int32, (SUBL, LANES), 0)
    n_i = RANKS // SUBL
    cols = [
        [x[i * SUBL : (i + 1) * SUBL, t * LANES : (t + 1) * LANES] for i in range(n_i)]
        for t in range(x.shape[1] // LANES)
    ]

    def permuted(v, index):
        return jnp.take_along_axis(v, index, axis=0)

    def joined(a, b):
        m = clean([jnp.maximum(a[i], permuted(b[n_i - 1 - i], SUBL - 1 - sublane)) for i in range(n_i)])
        d = SUBL // 2
        while d:
            near = (sublane & d) == 0
            for i in range(n_i):
                other = permuted(m[i], sublane ^ d)
                m[i] = jnp.where(near, jnp.maximum(m[i], other), jnp.minimum(m[i], other))
            d //= 2
        return m

    while len(cols) > 1:
        h = len(cols) // 2
        cols = [joined(cols[t], cols[t + h]) for t in range(h)]
    m = cols[0]
    width = LANES
    while width > rows:
        width //= 2
        m = joined(m, [pltpu.roll(v, width, 1) for v in m])
    out_ref[...] = jnp.concatenate(m, axis=0).T[:rows, :n_out]


def local(queries, codebook, probes, codes, part_sizes):
    n_dev = lax.axis_size("dom") * lax.axis_size("sub")
    own_rows, width = queries.shape
    n_probe = probes.shape[1]
    part_dev, groups, half = codes.shape
    n_cap = max(2, 2 * own_rows * n_probe // (part_dev * n_dev))
    chunks = 2
    chip_slots = part_dev * n_cap // chunks
    book = codebook.transpose(1, 2, 0)
    args = [pltpu.with_memory_space_constraint(x, pltpu.HBM) for x in (part_sizes, queries, probes.T, book, codes)]
    hbm = pl.BlockSpec(memory_space=pltpu.HBM)
    vmem, dma = pltpu.VMEM, pltpu.SemaphoreType.DMA
    lists = vmem((chunks, n_dev, chip_slots, RANKS), jnp.float32)
    rows = vmem((chunks, n_dev, chip_slots, width), jnp.bfloat16)
    decoded = vmem((part_dev, half, width), jnp.bfloat16)
    return pl.pallas_call(
        functools.partial(kernel, n_cap),
        out_shape=jax.ShapeDtypeStruct((own_rows, TOPK), jnp.float32),
        in_specs=[hbm] * 5,
        out_specs=pl.BlockSpec(memory_space=pltpu.VMEM),
        scratch_shapes=[
            pltpu.SMEM(part_sizes.shape, jnp.int32),
            vmem(queries.shape, jnp.bfloat16),
            vmem((n_probe, own_rows), jnp.int32),
            vmem(book.shape, jnp.bfloat16),
            rows,
            rows,
            vmem(codes.shape, jnp.int32),
            vmem((width, half), jnp.bfloat16),
            decoded,
            decoded,
            vmem((book.shape[1], groups, LANES), jnp.float32),
            vmem((part_dev // chunks, 256, n_dev * chip_slots), jnp.bfloat16),
            vmem((chunks, n_dev * chip_slots, n_probe * own_rows), jnp.bfloat16),
            vmem((2, 256, width), jnp.bfloat16),
            vmem((4, 2 * half // SUBL, SUBL, LANES), jnp.float32),
            vmem((4, RANKS, SUBL, LANES), jnp.float32),
            vmem((RANKS, SUBL, LANES), jnp.float32),
            vmem((RANKS * SUBL, LANES), jnp.float32),
            lists,
            lists,
            vmem((n_probe, own_rows), jnp.int32),
            dma((4,)),
            dma((part_dev,)),
            dma((part_dev,)),
            dma((part_dev,)),
            dma((chunks,)),
            dma((chunks,)),
            dma((chunks,)),
            dma((chunks,)),
            dma((chunks,)),
            dma((chunks,)),
        ],
        compiler_params=pltpu.CompilerParams(collective_id=0, has_side_effects=True, vmem_limit_bytes=40 << 20),
        name="search",
    )(*args)


def solution(mesh):
    in_specs = (
        P(("dom", "sub", "rep"), None),
        P(),
        P(("dom", "sub", "rep"), None),
        P(("dom", "sub"), None, "rep"),
        P(("dom", "sub")),
    )
    out_specs = P(("dom", "sub", "rep"), None)
    return jax.shard_map(local, mesh=mesh, in_specs=in_specs, out_specs=out_specs, check_vma=False)
```
